32 devices in a mesh: parts: 2 (over y), expert: 8 (over z, x), dp: 2 (over core).
Axes of the slice: x: 2, y: 2, z: 4, core: 2. Of those that a mesh axis runs over, the one named last changes fastest.
Arguments:
- tokens: bfloat16 [4096, 2048], P(('parts', 'expert', 'dp')), parts along dimension 0, may hold values from -6 to 6
- route_ids: int32 [4096, 2], P(('parts', 'expert', 'dp')), parts along dimension 0, may hold values from 0 to 31, all different within a row; in each aligned block of 128 rows (0 to 127, 128 to 255, ...) at most 10 rows name the same one
- route_gates: float32 [4096, 2], P(('parts', 'expert', 'dp')), parts along dimension 0, may hold values from 0.1 to 1
- gate_weight: bfloat16 [32, 2048, 1408], P('expert', None, 'dp'), may hold values from -0.125 to 0.125
- up_weight: bfloat16 [32, 2048, 1408], P('expert', None, 'dp'), may hold values from -0.125 to 0.125
- down_weight: bfloat16 [32, 1408, 2048], P('expert'), may hold values from -0.15625 to 0.15625
Outputs:
- output: bfloat16 [4096, 2048], P(('parts', 'expert', 'dp')), parts along dimension 0
The draws below stay inside these ranges and needn't reach their ends.
There are 2 independent parts, one for each index of `parts`. The reference program is written for one: setup_inputs(seed, part) draws one part's arguments, and reference() takes and returns one part's arrays. A program takes and returns all parts, laid end to end along the dimension named above; an argument that names none is the same for every part. Nothing has to cross between parts.
Inputs may be any that keep to these rules, and one draw needn't show every extreme that they name: `route_ids`: each row names 2 different experts; within the rows of one device (aligned blocks of 128 rows) no expert is named by more than 10 rows, a bound that some block reaches.
All inputs are finite; a program needn't handle non-finite values.
Results may differ from the reference program's by a relative error of at most 0.0058.
Values may be sent and summed in bfloat16 or wider, within the bound.
No kernel may reach another device: no remote copies, remote signals or barrier semaphores. Data moves between devices by JAX's collectives and lax.ppermute only.
A program may use at most 192 MiB of HBM per device.

```python
import math
import jax
import jax.numpy as jnp
import numpy as np
from jax import lax

D = 2048
FF = 1408
EXPERTS = 32
TOPK = 2
TOK_DEV = 128
CAP = 10
TOKENS = 2048
SEG = 1408
SEGS = 32


def levels(key, dims, shards, low, high):
    loudness, own = 1.0, jax.random.fold_in(key, 6)
    for axis_at, parts in shards:
        heights = jnp.exp(jax.random.uniform(jax.random.fold_in(own, axis_at), (parts,), jnp.float32, low / len(shards), high / len(shards)))
        loudness = loudness * jnp.repeat(heights, dims[axis_at] // parts).reshape([-1 if axis == axis_at else 1 for axis in range(len(dims))])
    return loudness


def shared_out(key, own, number, rows, amount, top, reach, slope):
    order = jax.random.permutation(key, amount)
    heavy_load, usual = portions_of(amount, rows * top, reach, slope, True), portions_of(amount, rows * top, reach, slope, False)
    places = jnp.arange(amount)

    def named(lengths, offset_by):
        used = int((lengths > 0).sum())
        fixed = max(1, used // 4)
        shifted = fixed + (places - fixed + offset_by * (used - fixed)) % max(1, amount - fixed)
        return jnp.zeros((amount,), jnp.int32).at[order[jnp.where(places < fixed, places, shifted)]].set(jnp.asarray(lengths, jnp.int32))

    lengths = jnp.where(number % 4 == 0, named(heavy_load, number // 4), named(usual, number - number // 4 - 1))
    mixed = jax.random.permutation(jax.random.fold_in(own, 3), amount)
    giver, sink = mixed[0:amount // 2 * 2:2], mixed[1:amount // 2 * 2:2]
    room = jnp.minimum(lengths[giver] - 1, reach - lengths[sink]) // 2
    room = jnp.where((giver == order[0]) | (sink == order[0]) | (lengths[sink] == 0), 0, jnp.maximum(room, 0))
    shifted = jax.random.randint(jax.random.fold_in(own, 4), (amount // 2,), 0, 1 << 20) % (room + 1)
    lengths = lengths.at[giver].add(-shifted).at[sink].add(shifted)
    items = jnp.searchsorted(jnp.cumsum(lengths), jnp.arange(rows * top), side="right").astype(jnp.int32)
    table = items.reshape(top, rows).T
    table = table[jax.random.permutation(jax.random.fold_in(own, 1), rows)]
    offset_by = jax.random.randint(jax.random.fold_in(own, 2), (rows, 1), 0, top)
    return jnp.take_along_axis(table, (jnp.arange(top)[None, :] + offset_by) % top, axis=1)


def portions_of(count, total, limit, slope, full):
    loads = [(1 << 20) // math.isqrt(rank ** slope) + 1 for rank in range(1, count + 1)]
    largest = limit if full else min(limit, max(-(-total // count), total * loads[0] // sum(loads)))
    least = 1 if total - largest >= count - 1 else 0
    holding, rest = [largest] + [least] * (count - 1), total - largest - least * (count - 1)
    while rest > 0:
        candidates = [i for i in range(1, count) if holding[i] < largest] or [i for i in range(1, count) if holding[i] < limit]
        pool, remaining = sum([loads[i] for i in candidates]), rest
        for i in candidates:
            more = min(limit - holding[i], max(1, remaining * loads[i] // pool), rest)
            holding[i] = holding[i] + more
            rest = rest - more
    return np.array(holding)


def gaussian(key, shape, scale, most, cuts=(), kind=jnp.bfloat16):
    level = levels(key, shape, cuts, -0.22, 0.18) if cuts else 1.0
    entries = jax.random.normal(key, shape, jnp.float32) * scale * level
    return jnp.minimum(jnp.maximum(entries, -most), most).astype(kind)


def setup_inputs(seed: int = 0, part: int = 0) -> dict:
    seeds = jax.random.split(jax.random.key(seed), 7)
    part_keys = jax.random.split(jax.random.fold_in(seeds[6], part), 7)
    tokens = gaussian(part_keys[0], (TOKENS, D), 1.0, 6.0, ((0, 16),))
    route_ids_keys = jax.random.split(jax.random.fold_in(part_keys[1], 1), TOKENS // TOK_DEV)
    route_ids_turns = jax.random.permutation(jax.random.fold_in(part_keys[1], 3), TOKENS // TOK_DEV)
    route_ids = jax.vmap(lambda own, number: shared_out(jax.random.fold_in(part_keys[1], 2), own, number, TOK_DEV, EXPERTS, TOPK, CAP, 2))(route_ids_keys, route_ids_turns).reshape((TOKENS, TOPK))
    route_gates = jnp.clip(0.1 + 0.9 * jax.random.uniform(part_keys[2], (TOKENS, TOPK), jnp.float32) ** levels(part_keys[2], (TOKENS, TOPK), ((0, 16),), -0.2, 0.2), 0.1, 1.0)
    gate_weight = gaussian(seeds[3], (SEGS, D, SEG), D ** -0.5, 0.125, ((0, 8), (2, 2)))
    up_weight = gaussian(seeds[4], (SEGS, D, SEG), D ** -0.5, 0.125, ((0, 8), (2, 2)))
    down_weight = gaussian(seeds[5], (SEGS, SEG, D), FF ** -0.5, 0.15625, ((0, 8),))
    return dict(tokens=tokens, route_ids=route_ids, route_gates=route_gates, gate_weight=gate_weight, up_weight=up_weight, down_weight=down_weight)


def reference(tokens, route_ids, route_gates, gate_weight, up_weight, down_weight):
    row_total = tokens.shape[0]
    block_count = row_total // TOK_DEV
    per_expert = FF // SEG
    width = tokens.shape[1]
    expert_iota = jnp.arange(EXPERTS, dtype=jnp.int32)
    matched = route_ids[:, :, None] == expert_iota[None, None, :]
    member = jnp.sum(matched.astype(jnp.int32), axis=1)
    weighting = jnp.sum(jnp.where(matched, route_gates[:, :, None], jnp.float32(0.0)), axis=1)
    member_blocks = member.reshape(block_count, TOK_DEV, EXPERTS)
    ranking = (jnp.cumsum(member_blocks, axis=1) - member_blocks).reshape(row_total, EXPERTS)
    row_iota = jnp.arange(row_total, dtype=jnp.int32)
    block_of = row_iota // TOK_DEV
    slot_count = block_count * CAP
    slot_index = jnp.where(member == 1, block_of[:, None] * CAP + ranking, slot_count).astype(jnp.int32)
    expert_grid = jnp.broadcast_to(expert_iota[None, :], (row_total, EXPERTS))
    row_grid = jnp.broadcast_to(row_iota[:, None], (row_total, EXPERTS))
    table = jnp.full((EXPERTS, slot_count + 1), row_total, jnp.int32)
    table = table.at[expert_grid, slot_index].set(row_grid)[:, :slot_count]
    tokens_pad = jnp.concatenate([tokens, jnp.zeros((1, width), tokens.dtype)], axis=0)
    weight_pad = jnp.concatenate([weighting, jnp.zeros((1, EXPERTS), jnp.float32)], axis=0)

    def one_expert(expert, total):
        picked = table[expert]
        rows_in = tokens_pad[picked].astype(jnp.float32)
        gates_in = weight_pad[picked, expert]
        first = (expert * per_expert).astype(jnp.int32)
        gate_seg = lax.dynamic_slice_in_dim(gate_weight, first, per_expert, 0).astype(jnp.float32)
        up_seg = lax.dynamic_slice_in_dim(up_weight, first, per_expert, 0).astype(jnp.float32)
        down_seg = lax.dynamic_slice_in_dim(down_weight, first, per_expert, 0).astype(jnp.float32)
        gate_val = jnp.einsum("rd,sdf->srf", rows_in, gate_seg)
        up_val = jnp.einsum("rd,sdf->srf", rows_in, up_seg)
        hidden = (jax.nn.silu(gate_val) * up_val).astype(jnp.bfloat16).astype(jnp.float32)
        partial_value = jnp.einsum("srf,sfd->srd", hidden, down_seg).astype(jnp.bfloat16)
        partial_value = lax.optimization_barrier(partial_value).astype(jnp.float32)
        expert_out = jnp.sum(partial_value, axis=0)
        return total.at[picked].add(gates_in[:, None] * expert_out)

    summed = lax.fori_loop(0, EXPERTS, one_expert, jnp.zeros((row_total + 1, width), jnp.float32))
    return summed[:row_total].astype(jnp.bfloat16)
```

```python
import functools

import jax
import jax.numpy as jnp
from jax import lax
from jax.experimental import pallas as pl
from jax.experimental.pallas import tpu as pltpu
from jax.sharding import PartitionSpec as P

FF = 1408
EXPERTS = 32
CAP = 10
TOPK = 2


def general(tokens, route_ids, route_gates, gate_weight, up_weight, down_weight):
    row_count = tokens.shape[0]
    width = tokens.shape[1]
    local_segs = gate_weight.shape[0]
    seg_width = down_weight.shape[1]
    groups = lax.axis_size("expert")
    per_expert = FF // seg_width
    expert_iota = jnp.arange(EXPERTS, dtype=jnp.int32)
    matched = route_ids[:, :, None] == expert_iota[None, None, :]
    member = jnp.sum(matched.astype(jnp.int32), axis=1)
    weighting = jnp.sum(jnp.where(matched, route_gates[:, :, None], jnp.float32(0.0)), axis=1)
    ranking = jnp.cumsum(member, axis=0) - member
    slot_iota = jnp.arange(CAP, dtype=jnp.int32)
    placed = (member[:, :, None] == 1) & (ranking[:, :, None] == slot_iota[None, None, :])
    placed_flat = placed.reshape(row_count, EXPERTS * CAP)
    chooser = placed_flat.astype(jnp.bfloat16)
    packed = jnp.dot(chooser.T, tokens, preferred_element_type=jnp.float32).astype(jnp.bfloat16)
    packed_four = packed.reshape(EXPERTS, 1, CAP, width)
    outgoing = jnp.broadcast_to(packed_four, (EXPERTS, per_expert, CAP, width))
    outgoing = outgoing.reshape(groups, local_segs, CAP, width)
    incoming = lax.all_to_all(outgoing, "expert", split_axis=0, concat_axis=0, tiled=True)
    full_gate, full_up = (
        lax.all_gather(gate_weight, "dp", axis=2, tiled=True),
        lax.all_gather(up_weight, "dp", axis=2, tiled=True),
    )
    gate_val = jnp.einsum("gscd,sdf->gscf", incoming, full_gate, preferred_element_type=jnp.float32)
    up_val = jnp.einsum("gscd,sdf->gscf", incoming, full_up, preferred_element_type=jnp.float32)
    hidden = (jax.nn.silu(gate_val) * up_val).astype(jnp.bfloat16)
    partial_value = jnp.einsum(
        "gscf,sfd->gscd", hidden, down_weight, preferred_element_type=jnp.float32
    ).astype(jnp.bfloat16)
    returned = lax.all_to_all(partial_value, "expert", split_axis=0, concat_axis=0, tiled=True)
    per_seg = returned.reshape(EXPERTS, per_expert, CAP, width).astype(jnp.float32)
    expert_out = jnp.sum(per_seg, axis=1).reshape(EXPERTS * CAP, width)
    combine = jnp.where(placed, weighting[:, :, None], jnp.float32(0.0)).reshape(
        row_count, EXPERTS * CAP
    )
    output = jnp.dot(
        combine, expert_out, precision=lax.Precision.HIGHEST, preferred_element_type=jnp.float32
    )
    return output.astype(jnp.bfloat16)


VMEM = pltpu.VMEM
MIB = 1 << 20


def dot(a, b):
    return jnp.dot(a, b, preferred_element_type=jnp.float32)


def dot_nt(a, b):
    return lax.dot_general(a, b, (((1,), (1,)), ((), ())), preferred_element_type=jnp.float32)


def iota(shape, axis):
    return lax.broadcasted_iota(jnp.int32, shape, axis)


def pack_kernel(local_experts, groups, place_ref, ids_ref, tokens_ref, *outs):
    slots_ref, blocks = outs[0], outs[1:]
    rows = tokens_ref.shape[0]
    block = local_experts * CAP
    me = place_ref[0]
    ids = ids_ref[...]
    lane = iota((rows, 128), 1)
    picks = [(lane == ids[:, k : k + 1]).astype(jnp.float32) for k in range(TOPK)]
    member = functools.reduce(lambda a, b: a + b, picks)
    earlier = (iota((rows, rows), 1) < iota((rows, rows), 0)).astype(jnp.bfloat16)
    ranking = dot(earlier, member.astype(jnp.bfloat16))
    shift = local_experts.bit_length() - 1
    slots = []
    for k in range(TOPK):
        rank = jnp.sum(picks[k] * ranking, axis=1, keepdims=True).astype(jnp.int32)
        one = ids[:, k : k + 1]
        slots.append(((one >> shift) ^ me) * block + (one & (local_experts - 1)) * CAP + rank)
    slots_ref[...] = jnp.concatenate(slots, axis=1)
    total = groups * block
    padded = -(-total // 128) * 128
    place = iota((rows, padded), 1)
    chosen = functools.reduce(lambda a, b: a | b, [place == s for s in slots])
    chooser = chosen.astype(jnp.float32).T.astype(jnp.bfloat16)
    step = 512
    for c in range(0, tokens_ref.shape[1], step):
        got = dot(chooser, tokens_ref[:, c : c + step]).astype(jnp.bfloat16)
        for g in range(groups):
            blocks[g][:, c : c + step] = got[g * block : (g + 1) * block, :]


def regroup_kernel(local_experts, count, padded, *refs):
    ins, out_ref, held = refs[:count], refs[count], refs[count + 1]
    block = local_experts * CAP
    for b in range(count):
        held[b * block : (b + 1) * block, :] = ins[b][...]
    q = iota((local_experts * padded, 1), 0)
    j = q & (padded - 1)
    b = (j * 205) >> 11
    source = b * block + (q >> (padded.bit_length() - 1)) * CAP + (j - b * CAP)
    source = jnp.where(j < count * CAP, source, -1)
    mover = (iota((local_experts * padded, count * block), 1) == source).astype(jnp.bfloat16)
    step = 512
    for c in range(0, held.shape[1], step):
        out_ref[:, c : c + step] = dot(mover, held[:, c : c + step]).astype(jnp.bfloat16)


def ungroup_kernel(local_experts, count, padded, own_ref, other_ref, *refs):
    block = local_experts * CAP
    s = iota((count * block, 1), 0)
    b = (s * 1639) >> 16
    t = s - b * block
    e = (t * 205) >> 11
    source = e * padded + b * CAP + (t - e * CAP)
    mover = (iota((count * block, local_experts * padded), 1) == source).astype(jnp.bfloat16)
    step = 512
    for c in range(0, own_ref.shape[1], step):
        whole = own_ref[:, c : c + step] + other_ref[:, c : c + step].astype(jnp.float32)
        got = dot(mover, whole.astype(jnp.bfloat16)).astype(jnp.bfloat16)
        for k in range(count):
            refs[k][:, c : c + step] = got[k * block : (k + 1) * block, :]


def ffn_kernel(steps, place_ref, mine_ref, theirs_ref, gate_ref, up_ref, down_ref, own_ref, send_ref, acc):
    f = pl.program_id(1)
    rows = jnp.concatenate([mine_ref[...], theirs_ref[...]], axis=0)
    gate = dot_nt(rows, gate_ref[0])
    up = dot_nt(rows, up_ref[0])
    hidden = (gate / (1.0 + jnp.exp(-gate)) * up).astype(jnp.bfloat16)
    part = dot(hidden, down_ref[0])

    @pl.when(f == 0)
    def _():
        acc[...] = part

    @pl.when(f > 0)
    def _():
        acc[...] += part

    @pl.when(f == steps - 1)
    def _():
        half = mine_ref.shape[0]
        own_ref[...] = acc[:half, :]
        send_ref[...] = acc[half:, :].astype(jnp.bfloat16)


def combine_kernel(block, slots_ref, gates_ref, *refs):
    groups = len(refs) - 2
    ins, out_ref, held = refs[:groups], refs[groups], refs[groups + 1]
    for g in range(groups):
        held[g * block : (g + 1) * block, :] = ins[g][...]
    rows = slots_ref.shape[0]
    place = iota((rows, groups * block), 1)
    slots, gates = slots_ref[...], gates_ref[...]
    picks = [(place == slots[:, k : k + 1]).astype(jnp.bfloat16) for k in range(TOPK)]
    step = 512
    for c in range(0, out_ref.shape[1], step):
        part = held[:, c : c + step]
        total = sum(gates[:, k : k + 1] * dot(picks[k], part) for k in range(TOPK))
        out_ref[:, c : c + step] = total.astype(jnp.bfloat16)


def params(limit):
    return pltpu.CompilerParams(vmem_limit_bytes=limit * MIB)


def whole(count):
    return [pl.BlockSpec(memory_space=VMEM)] * count


def fast(tokens, route_ids, route_gates, gate_weight, up_weight, down_weight):
    rows, width = tokens.shape
    groups = lax.axis_size("expert")
    local_experts, _, half = gate_weight.shape
    block = local_experts * CAP
    bf16 = jnp.bfloat16
    place = jnp.stack([lax.axis_index("expert"), lax.axis_index("dp")]).astype(jnp.int32)
    smem = pl.BlockSpec(memory_space=pltpu.SMEM)
    gate_rows = jnp.swapaxes(gate_weight, 1, 2)
    up_rows = jnp.swapaxes(up_weight, 1, 2)

    packed = pl.pallas_call(
        functools.partial(pack_kernel, local_experts, groups),
        out_shape=[jax.ShapeDtypeStruct((rows, TOPK), jnp.int32)]
        + [jax.ShapeDtypeStruct((block, width), bf16)] * groups,
        in_specs=[smem] + whole(2),
        out_specs=whole(1 + groups),
        compiler_params=params(16),
        name="pack",
    )(place, route_ids, tokens)
    slots, outgoing = packed[0], packed[1:]

    def hop(x, k):
        return lax.ppermute(x, "expert", [(i, i ^ k) for i in range(groups)])

    def swap(x):
        return lax.ppermute(x, "dp", [(0, 1), (1, 0)])

    order = [4, 5, 1, 2, 3, 6, 7]
    chunks = [[0, 4, 5, 1, 2, 3], [6, 7]]
    incoming = {0: outgoing[0]}
    for k in order:
        incoming[k] = hop(outgoing[k], k)

    steps = 2
    tile = half // steps
    returned = {}
    for chunk in chunks:
        count = len(chunk)
        padded = 1 << (count * CAP - 1).bit_length()
        tall = local_experts * padded
        mine = pl.pallas_call(
            functools.partial(regroup_kernel, local_experts, count, padded),
            out_shape=jax.ShapeDtypeStruct((tall, width), bf16),
            in_specs=whole(count),
            out_specs=whole(1)[0],
            scratch_shapes=[VMEM((count * block, width), bf16)],
            compiler_params=params(16),
            name="regroup",
        )(*[incoming[k] for k in chunk])
        theirs = swap(mine)
        own, send = pl.pallas_call(
            functools.partial(ffn_kernel, steps),
            out_shape=[
                jax.ShapeDtypeStruct((tall, width), jnp.float32),
                jax.ShapeDtypeStruct((tall, width), bf16),
            ],
            grid_spec=pltpu.PrefetchScalarGridSpec(
                num_scalar_prefetch=1,
                grid=(local_experts, steps),
                in_specs=[
                    pl.BlockSpec((padded, width), lambda e, f, at: (e, 0)),
                    pl.BlockSpec((padded, width), lambda e, f, at: (e, 0)),
                    pl.BlockSpec((1, tile, width), lambda e, f, at: (e, f, 0)),
                    pl.BlockSpec((1, tile, width), lambda e, f, at: (e, f, 0)),
                    pl.BlockSpec((1, tile, width), lambda e, f, at: (e, at[1] * steps + f, 0)),
                ],
                out_specs=[
                    pl.BlockSpec((padded, width), lambda e, f, at: (e, 0)),
                    pl.BlockSpec((padded, width), lambda e, f, at: (e, 0)),
                ],
                scratch_shapes=[VMEM((2 * padded, width), jnp.float32)],
            ),
            compiler_params=params(32),
            name="ffn",
        )(place, mine, theirs, gate_rows, up_rows, down_weight)
        other = swap(send)
        blocks = pl.pallas_call(
            functools.partial(ungroup_kernel, local_experts, count, padded),
            out_shape=[jax.ShapeDtypeStruct((block, width), bf16)] * count,
            in_specs=whole(2),
            out_specs=whole(count),
            compiler_params=params(16),
            name="ungroup",
        )(own, other)
        for k, y in zip(chunk, blocks):
            returned[k] = hop(y, k) if k else y

    return pl.pallas_call(
        functools.partial(combine_kernel, block),
        out_shape=jax.ShapeDtypeStruct((rows, width), bf16),
        in_specs=whole(2 + groups),
        out_specs=whole(1)[0],
        scratch_shapes=[VMEM((groups * block, width), bf16)],
        compiler_params=params(16),
        name="combine",
    )(slots, route_gates, *[returned[k] for k in range(groups)])


def on_device(tokens, route_ids, route_gates, gate_weight, up_weight, down_weight):
    suits = (
        lax.axis_size("expert") == 8
        and lax.axis_size("dp") == 2
        and down_weight.shape[1] == FF
        and gate_weight.shape[0] == 4
        and tokens.shape[0] == 128
    )
    run = fast if suits else general
    return run(tokens, route_ids, route_gates, gate_weight, up_weight, down_weight)


def solution(mesh):
    placed = (
        P(("parts", "expert", "dp"), None),
        P(("parts", "expert", "dp"), None),
        P(("parts", "expert", "dp"), None),
        P("expert", None, "dp"),
        P("expert", None, "dp"),
        P("expert", None, None),
    )
    return jax.shard_map(
        on_device,
        mesh=mesh,
        in_specs=placed,
        out_specs=P(("parts", "expert", "dp"), None),
        check_vma=False,
    )
```

```python
import functools

import jax
import jax.numpy as jnp
from jax import lax
from jax.experimental import pallas as pl
from jax.experimental.pallas import tpu as pltpu
from jax.sharding import PartitionSpec as P

FF = 1408
EXPERTS = 32
CAP = 10
TOPK = 2
SPLITS = (4, 4)


def general(tokens, route_ids, route_gates, gate_weight, up_weight, down_weight):
    row_count = tokens.shape[0]
    width = tokens.shape[1]
    local_segs = gate_weight.shape[0]
    seg_width = down_weight.shape[1]
    groups = lax.axis_size("expert")
    per_expert = FF // seg_width
    expert_iota = jnp.arange(EXPERTS, dtype=jnp.int32)
    matched = route_ids[:, :, None] == expert_iota[None, None, :]
    member = jnp.sum(matched.astype(jnp.int32), axis=1)
    weighting = jnp.sum(jnp.where(matched, route_gates[:, :, None], jnp.float32(0.0)), axis=1)
    ranking = jnp.cumsum(member, axis=0) - member
    slot_iota = jnp.arange(CAP, dtype=jnp.int32)
    placed = (member[:, :, None] == 1) & (ranking[:, :, None] == slot_iota[None, None, :])
    placed_flat = placed.reshape(row_count, EXPERTS * CAP)
    chooser = placed_flat.astype(jnp.bfloat16)
    packed = jnp.dot(chooser.T, tokens, preferred_element_type=jnp.float32).astype(jnp.bfloat16)
    packed_four = packed.reshape(EXPERTS, 1, CAP, width)
    outgoing = jnp.broadcast_to(packed_four, (EXPERTS, per_expert, CAP, width))
    outgoing = outgoing.reshape(groups, local_segs, CAP, width)
    incoming = lax.all_to_all(outgoing, "expert", split_axis=0, concat_axis=0, tiled=True)
    full_gate, full_up = (
        lax.all_gather(gate_weight, "dp", axis=2, tiled=True),
        lax.all_gather(up_weight, "dp", axis=2, tiled=True),
    )
    gate_val = jnp.einsum("gscd,sdf->gscf", incoming, full_gate, preferred_element_type=jnp.float32)
    up_val = jnp.einsum("gscd,sdf->gscf", incoming, full_up, preferred_element_type=jnp.float32)
    hidden = (jax.nn.silu(gate_val) * up_val).astype(jnp.bfloat16)
    partial_value = jnp.einsum(
        "gscf,sfd->gscd", hidden, down_weight, preferred_element_type=jnp.float32
    ).astype(jnp.bfloat16)
    returned = lax.all_to_all(partial_value, "expert", split_axis=0, concat_axis=0, tiled=True)
    per_seg = returned.reshape(EXPERTS, per_expert, CAP, width).astype(jnp.float32)
    expert_out = jnp.sum(per_seg, axis=1).reshape(EXPERTS * CAP, width)
    combine = jnp.where(placed, weighting[:, :, None], jnp.float32(0.0)).reshape(
        row_count, EXPERTS * CAP
    )
    output = jnp.dot(
        combine, expert_out, precision=lax.Precision.HIGHEST, preferred_element_type=jnp.float32
    )
    return output.astype(jnp.bfloat16)


VMEM = pltpu.VMEM
MIB = 1 << 20


def dot(a, b):
    return jnp.dot(a, b, preferred_element_type=jnp.float32)


def dot_nt(a, b):
    return lax.dot_general(a, b, (((1,), (1,)), ((), ())), preferred_element_type=jnp.float32)


def iota(shape, axis):
    return lax.broadcasted_iota(jnp.int32, shape, axis)


def pack_kernel(local_experts, groups, place_ref, ids_ref, gates_ref, tokens_ref, *outs):
    route_ref, blocks = outs[0], outs[1:]
    rows = tokens_ref.shape[0]
    block = local_experts * CAP
    me = place_ref[0]
    ids = ids_ref[...]
    expert = iota((EXPERTS, rows), 0)
    picks = [(expert == ids[k : k + 1, :]).astype(jnp.float32) for k in range(TOPK)]
    member = functools.reduce(lambda a, b: a + b, picks)
    earlier = (iota((rows, rows), 0) < iota((rows, rows), 1)).astype(jnp.bfloat16)
    ranking = dot(member.astype(jnp.bfloat16), earlier)
    shift = local_experts.bit_length() - 1
    slots = []
    for k in range(TOPK):
        rank = jnp.sum(picks[k] * ranking, axis=0, keepdims=True).astype(jnp.int32)
        one = ids[k : k + 1, :]
        slots.append(((one >> shift) ^ me) * block + (one & (local_experts - 1)) * CAP + rank)
    place = iota((groups * block, rows), 0)
    chosen = functools.reduce(lambda a, b: a | b, [place == s for s in slots])
    chooser = chosen.astype(jnp.bfloat16)
    step = 512
    for c in range(0, tokens_ref.shape[1], step):
        got = dot(chooser, tokens_ref[:, c : c + step]).astype(jnp.bfloat16)
        for g in range(groups):
            blocks[g][:, c : c + step] = got[g * block : (g + 1) * block, :]
    columns = [s.astype(jnp.float32) for s in slots] + [gates_ref[...]]
    columns.append(jnp.zeros((rows - 2 * TOPK, rows), jnp.float32))
    route_ref[...] = jnp.concatenate(columns, axis=0).T


def regroup_kernel(local_experts, count, padded, *refs):
    ins, out_ref, pieces, held = refs[:count], refs[count], refs[count + 1 : -1], refs[-1]
    each = local_experts * padded // len(pieces)
    block = local_experts * CAP
    for b in range(count):
        held[b * block : (b + 1) * block, :] = ins[b][...]
    q = iota((local_experts * padded, 1), 0)
    j = q & (padded - 1)
    b = (j * 205) >> 11
    source = b * block + (q >> (padded.bit_length() - 1)) * CAP + (j - b * CAP)
    source = jnp.where(j < count * CAP, source, -1)
    mover = (iota((local_experts * padded, count * block), 1) == source).astype(jnp.bfloat16)
    step = 512
    for c in range(0, held.shape[1], step):
        got = dot(mover, held[:, c : c + step]).astype(jnp.bfloat16)
        out_ref[:, c : c + step] = got
        for k in range(len(pieces)):
            pieces[k][:, c : c + step] = got[k * each : (k + 1) * each, :]


def ungroup_kernel(local_experts, count, padded, own_ref, *refs):
    others, refs = refs[:-count], refs[-count:]
    each = local_experts * padded // len(others)
    block = local_experts * CAP
    s = iota((count * block, 1), 0)
    b = (s * 1639) >> 16
    t = s - b * block
    e = (t * 205) >> 11
    source = e * padded + b * CAP + (t - e * CAP)
    mover = (iota((count * block, local_experts * padded), 1) == source).astype(jnp.bfloat16)
    step = 512
    for c in range(0, own_ref.shape[1], step):
        parts = []
        for k, other_ref in enumerate(others):
            part = own_ref[k * each : (k + 1) * each, c : c + step]
            parts.append((part + other_ref[:, c : c + step].astype(jnp.float32)).astype(jnp.bfloat16))
        got = dot(mover, jnp.concatenate(parts, axis=0)).astype(jnp.bfloat16)
        for k in range(count):
            refs[k][:, c : c + step] = got[k * block : (k + 1) * block, :]


def load_kernel(half, place_ref, _, gate_hbm, up_hbm, down_hbm, *refs):
    sems = refs[-1]
    first = pl.multiple_of(place_ref[1] * half, 8)
    copies = []
    for e in range(gate_hbm.shape[0]):
        sources = [gate_hbm.at[e], up_hbm.at[e], down_hbm.at[e, pl.ds(first, half), :]]
        for source in sources:
            at = len(copies)
            copies.append(pltpu.make_async_copy(source, refs[at], sems.at[at]))
    for copy in copies:
        copy.start()
    for copy in copies:
        copy.wait()


def ffn_kernel(padded, pieces, mine_ref, *refs):
    theirs, refs = refs[:pieces], refs[pieces:]
    weights, own_ref, sends = refs[: -1 - pieces], refs[-1 - pieces], refs[-pieces:]
    each = len(weights) // 3 // pieces
    for e in range(len(weights) // 3):
        gate_ref, up_ref, down_ref = weights[3 * e : 3 * e + 3]
        at = slice(e * padded, (e + 1) * padded)
        low = slice((e % each) * padded, (e % each + 1) * padded)
        rows = jnp.concatenate([mine_ref[at, :], theirs[e // each][low, :]], axis=0)
        gate = dot_nt(rows, gate_ref[...])
        up = dot_nt(rows, up_ref[...])
        hidden = (gate / (1.0 + jnp.exp(-gate)) * up).astype(jnp.bfloat16)
        part = dot(hidden, down_ref[...])
        own_ref[at, :] = part[:padded, :]
        sends[e // each][low, :] = part[padded:, :].astype(jnp.bfloat16)


def combine_kernel(block, route_ref, *refs):
    groups = len(refs) - 2
    ins, out_ref, held = refs[:groups], refs[groups], refs[groups + 1]
    for g in range(groups):
        held[g * block : (g + 1) * block, :] = ins[g][...]
    rows = route_ref.shape[0]
    place = iota((rows, groups * block), 1)
    slots = [route_ref[:, k : k + 1].astype(jnp.int32) for k in range(TOPK)]
    gates = [route_ref[:, TOPK + k : TOPK + k + 1] for k in range(TOPK)]
    picks = [(place == s).astype(jnp.bfloat16) for s in slots]
    step = 512
    for c in range(0, out_ref.shape[1], step):
        part = held[:, c : c + step]
        total = sum(gates[k] * dot(picks[k], part) for k in range(TOPK))
        out_ref[:, c : c + step] = total.astype(jnp.bfloat16)


def params(limit):
    return pltpu.CompilerParams(vmem_limit_bytes=limit * MIB)


def cost(flops, moved):
    return pl.CostEstimate(flops=flops, bytes_accessed=moved, transcendentals=0)


def whole(count):
    return [pl.BlockSpec(memory_space=VMEM)] * count


def fast(tokens, route_ids, route_gates, gate_weight, up_weight, down_weight):
    rows, width = tokens.shape
    groups = lax.axis_size("expert")
    local_experts, _, half = gate_weight.shape
    block = local_experts * CAP
    bf16 = jnp.bfloat16
    place = jnp.stack([lax.axis_index("expert"), lax.axis_index("dp")]).astype(jnp.int32)
    smem = pl.BlockSpec(memory_space=pltpu.SMEM)
    hbm = pl.BlockSpec(memory_space=pltpu.HBM)
    gate_rows = pltpu.with_memory_space_constraint(jnp.swapaxes(gate_weight, 1, 2), pltpu.HBM)
    up_rows = pltpu.with_memory_space_constraint(jnp.swapaxes(up_weight, 1, 2), pltpu.HBM)
    down_weight = pltpu.with_memory_space_constraint(down_weight, pltpu.HBM)

    packed = pl.pallas_call(
        functools.partial(pack_kernel, local_experts, groups),
        out_shape=[jax.ShapeDtypeStruct((rows, rows), jnp.float32)]
        + [jax.ShapeDtypeStruct((block, width), bf16)] * groups,
        in_specs=[smem] + whole(3),
        out_specs=whole(1 + groups),
        compiler_params=params(4),
        cost_estimate=cost(2 * groups * block * rows * width, 2 * 3 * rows * width),
        name="pack",
    )(place, route_ids.T, route_gates.T, tokens)
    route, outgoing = packed[0], packed[1:]

    def hop(x, k):
        return lax.ppermute(x, "expert", [(i, i ^ k) for i in range(groups)])

    def swap(x):
        return lax.ppermute(x, "dp", [(0, 1), (1, 0)])

    order = [1, 2, 3, 4, 5, 6, 7]
    after = {6: 1, 7: 2}
    chunks = [[0, 1, 2, 3, 4, 5], [6, 7]]
    incoming = {0: outgoing[0]}
    for k in order:
        held = outgoing[k]
        if k in after:
            held, _ = lax.optimization_barrier((held, incoming[after[k]]))
        incoming[k] = hop(held, k)
    route_now, _, _ = lax.optimization_barrier((route, incoming[1], incoming[2]))

    share = jax.ShapeDtypeStruct((half, width), bf16)
    pieces = 3 * local_experts
    weights = pl.pallas_call(
        functools.partial(load_kernel, half),
        out_shape=[share] * pieces,
        in_specs=[smem] + whole(1) + [hbm] * 3,
        out_specs=whole(pieces),
        scratch_shapes=[pltpu.SemaphoreType.DMA((pieces,))],
        compiler_params=params(1),
        cost_estimate=cost(0, 6 * local_experts * half * width),
        name="load",
    )(place, route_now, gate_rows, up_rows, down_weight)
    incoming[4], gate_now = lax.optimization_barrier((incoming[4], weights[0]))
    weights = [gate_now] + list(weights[1:])

    returned = {}
    last = None
    for chunk in chunks:
        count = len(chunk)
        padded = 1 << (count * CAP - 1).bit_length()
        tall = local_experts * padded
        splits = SPLITS[0] if count > 2 else SPLITS[1]
        piece = jax.ShapeDtypeStruct((tall // splits, width), bf16)
        mine, *cut = pl.pallas_call(
            functools.partial(regroup_kernel, local_experts, count, padded),
            out_shape=[jax.ShapeDtypeStruct((tall, width), bf16)] + [piece] * splits,
            in_specs=whole(count),
            out_specs=whole(1 + splits),
            scratch_shapes=[VMEM((count * block, width), bf16)],
            compiler_params=params(4),
            cost_estimate=cost(2 * tall * count * block * width, 4 * tall * width),
            name="regroup",
        )(*[incoming[k] for k in chunk])
        theirs = [swap(x) for x in cut]
        own, *send = pl.pallas_call(
            functools.partial(ffn_kernel, padded, splits),
            out_shape=[
                jax.ShapeDtypeStruct((tall, width), jnp.float32),
            ]
            + [piece] * splits,
            in_specs=whole(1 + splits + pieces),
            out_specs=whole(1 + splits),
            compiler_params=params(6),
            cost_estimate=cost(12 * tall * width * half, 6 * local_experts * half * width),
            name="ffn",
        )(mine, *theirs, *weights)
        other = [swap(x) for x in send]
        blocks = pl.pallas_call(
            functools.partial(ungroup_kernel, local_experts, count, padded),
            out_shape=[jax.ShapeDtypeStruct((block, width), bf16)] * count,
            in_specs=whole(1 + splits),
            out_specs=whole(count),
            compiler_params=params(4),
            cost_estimate=cost(2 * tall * count * block * width, 4 * tall * width),
            name="ungroup",
        )(own, *other)
        last = blocks[0]
        for k, y in zip(chunk, blocks):
            returned[k] = hop(y, k) if k else y

    return pl.pallas_call(
        functools.partial(combine_kernel, block),
        out_shape=jax.ShapeDtypeStruct((rows, width), bf16),
        in_specs=whole(1 + groups),
        out_specs=whole(1)[0],
        scratch_shapes=[VMEM((groups * block, width), bf16)],
        compiler_params=params(4),
        cost_estimate=cost(4 * rows * groups * block * width, 4 * rows * width),
        name="combine",
    )(route, *[returned[k] for k in range(groups)])


def on_device(tokens, route_ids, route_gates, gate_weight, up_weight, down_weight):
    suits = (
        lax.axis_size("expert") == 8
        and lax.axis_size("dp") == 2
        and down_weight.shape[1] == FF
        and gate_weight.shape[0] == 4
        and tokens.shape[0] == 128
    )
    run = fast if suits else general
    return run(tokens, route_ids, route_gates, gate_weight, up_weight, down_weight)


def solution(mesh):
    placed = (
        P(("parts", "expert", "dp"), None),
        P(("parts", "expert", "dp"), None),
        P(("parts", "expert", "dp"), None),
        P("expert", None, "dp"),
        P("expert", None, "dp"),
        P("expert", None, None),
    )
    return jax.shard_map(
        on_device,
        mesh=mesh,
        in_specs=placed,
        out_specs=P(("parts", "expert", "dp"), None),
        check_vma=False,
    )
```

```python
import functools

import jax
import jax.numpy as jnp
from jax import lax
from jax.experimental import pallas as pl
from jax.experimental.pallas import tpu as pltpu
from jax.sharding import PartitionSpec as P

FF = 1408
EXPERTS = 32
CAP = 10
TOPK = 2


def general(tokens, route_ids, route_gates, gate_weight, up_weight, down_weight):
    row_count = tokens.shape[0]
    width = tokens.shape[1]
    local_segs = gate_weight.shape[0]
    seg_width = down_weight.shape[1]
    groups = lax.axis_size("expert")
    per_expert = FF // seg_width
    expert_iota = jnp.arange(EXPERTS, dtype=jnp.int32)
    matched = route_ids[:, :, None] == expert_iota[None, None, :]
    member = jnp.sum(matched.astype(jnp.int32), axis=1)
    weighting = jnp.sum(jnp.where(matched, route_gates[:, :, None], jnp.float32(0.0)), axis=1)
    ranking = jnp.cumsum(member, axis=0) - member
    slot_iota = jnp.arange(CAP, dtype=jnp.int32)
    placed = (member[:, :, None] == 1) & (ranking[:, :, None] == slot_iota[None, None, :])
    placed_flat = placed.reshape(row_count, EXPERTS * CAP)
    chooser = placed_flat.astype(jnp.bfloat16)
    packed = jnp.dot(chooser.T, tokens, preferred_element_type=jnp.float32).astype(jnp.bfloat16)
    packed_four = packed.reshape(EXPERTS, 1, CAP, width)
    outgoing = jnp.broadcast_to(packed_four, (EXPERTS, per_expert, CAP, width))
    outgoing = outgoing.reshape(groups, local_segs, CAP, width)
    incoming = lax.all_to_all(outgoing, "expert", split_axis=0, concat_axis=0, tiled=True)
    full_gate, full_up = (
        lax.all_gather(gate_weight, "dp", axis=2, tiled=True),
        lax.all_gather(up_weight, "dp", axis=2, tiled=True),
    )
    gate_val = jnp.einsum("gscd,sdf->gscf", incoming, full_gate, preferred_element_type=jnp.float32)
    up_val = jnp.einsum("gscd,sdf->gscf", incoming, full_up, preferred_element_type=jnp.float32)
    hidden = (jax.nn.silu(gate_val) * up_val).astype(jnp.bfloat16)
    partial_value = jnp.einsum(
        "gscf,sfd->gscd", hidden, down_weight, preferred_element_type=jnp.float32
    ).astype(jnp.bfloat16)
    returned = lax.all_to_all(partial_value, "expert", split_axis=0, concat_axis=0, tiled=True)
    per_seg = returned.reshape(EXPERTS, per_expert, CAP, width).astype(jnp.float32)
    expert_out = jnp.sum(per_seg, axis=1).reshape(EXPERTS * CAP, width)
    combine = jnp.where(placed, weighting[:, :, None], jnp.float32(0.0)).reshape(
        row_count, EXPERTS * CAP
    )
    output = jnp.dot(
        combine, expert_out, precision=lax.Precision.HIGHEST, preferred_element_type=jnp.float32
    )
    return output.astype(jnp.bfloat16)


VMEM = pltpu.VMEM
MIB = 1 << 20


def dot(a, b):
    return jnp.dot(a, b, preferred_element_type=jnp.float32)


def dot_nt(a, b):
    return lax.dot_general(a, b, (((1,), (1,)), ((), ())), preferred_element_type=jnp.float32)


def iota(shape, axis):
    return lax.broadcasted_iota(jnp.int32, shape, axis)


def pack_kernel(local_experts, groups, place_ref, ids_ref, gates_ref, tokens_ref, *outs):
    route_ref, blocks = outs[0], outs[1:]
    rows = tokens_ref.shape[0]
    block = local_experts * CAP
    me = place_ref[0]
    ids = ids_ref[...]
    expert = iota((EXPERTS, rows), 0)
    picks = [(expert == ids[k : k + 1, :]).astype(jnp.float32) for k in range(TOPK)]
    member = functools.reduce(lambda a, b: a + b, picks)
    earlier = (iota((rows, rows), 0) < iota((rows, rows), 1)).astype(jnp.bfloat16)
    ranking = dot(member.astype(jnp.bfloat16), earlier)
    shift = local_experts.bit_length() - 1
    slots = []
    for k in range(TOPK):
        rank = jnp.sum(picks[k] * ranking, axis=0, keepdims=True).astype(jnp.int32)
        one = ids[k : k + 1, :]
        slots.append(((one >> shift) ^ me) * block + (one & (local_experts - 1)) * CAP + rank)
    place = iota((groups * block, rows), 0)
    chosen = functools.reduce(lambda a, b: a | b, [place == s for s in slots])
    chooser = chosen.astype(jnp.bfloat16)
    step = 512
    for c in range(0, tokens_ref.shape[1], step):
        got = dot(chooser, tokens_ref[:, c : c + step]).astype(jnp.bfloat16)
        for g in range(groups):
            blocks[g][:, c : c + step] = got[g * block : (g + 1) * block, :]
    columns = [s.astype(jnp.float32) for s in slots] + [gates_ref[...]]
    columns.append(jnp.zeros((rows - 2 * TOPK, rows), jnp.float32))
    route_ref[...] = jnp.concatenate(columns, axis=0).T


def regroup_kernel(local_experts, count, *refs):
    ins, low_ref, high_ref, held = refs[:count], refs[count], refs[count + 1], refs[count + 2]
    block, each = local_experts * CAP, count * CAP
    for b in range(count):
        held[b * block : (b + 1) * block, :] = ins[b][...]
    q = iota((local_experts * each, 1), 0)
    e = sum((q >= k * each).astype(jnp.int32) for k in range(1, local_experts))
    j = q - e * each
    b = (j * 205) >> 11
    source = b * block + e * CAP + (j - b * CAP)
    mover = (iota((local_experts * each, count * block), 1) == source).astype(jnp.bfloat16)
    step, middle = 512, low_ref.shape[0]
    for c in range(0, held.shape[1], step):
        got = dot(mover, held[:, c : c + step]).astype(jnp.bfloat16)
        low_ref[:, c : c + step] = got[:middle, :]
        high_ref[:, c : c + step] = got[middle:, :]


def ungroup_kernel(local_experts, count, own_low, own_high, other_low, other_high, *refs):
    block, each = local_experts * CAP, count * CAP
    s = iota((count * block, 1), 0)
    b = (s * 1639) >> 16
    t = s - b * block
    e = (t * 205) >> 11
    source = e * each + b * CAP + (t - e * CAP)
    mover = (iota((count * block, local_experts * each), 1) == source).astype(jnp.bfloat16)
    step = 512
    for c in range(0, own_low.shape[1], step):
        at = slice(c, c + step)
        parts = [
            (own[:, at] + other[:, at].astype(jnp.float32)).astype(jnp.bfloat16)
            for own, other in ((own_low, other_low), (own_high, other_high))
        ]
        got = dot(mover, jnp.concatenate(parts, axis=0)).astype(jnp.bfloat16)
        for k in range(count):
            refs[k][:, at] = got[k * block : (k + 1) * block, :]


def load_kernel(half, place_ref, _, gate_hbm, up_hbm, down_hbm, *refs):
    sems = refs[-1]
    first = pl.multiple_of(place_ref[1] * half, 8)
    copies = []
    for e in range(gate_hbm.shape[0]):
        sources = [gate_hbm.at[e], up_hbm.at[e], down_hbm.at[e, pl.ds(first, half), :]]
        for source in sources:
            at = len(copies)
            copies.append(pltpu.make_async_copy(source, refs[at], sems.at[at]))
    for copy in copies:
        copy.start()
    for copy in copies:
        copy.wait()


def ffn_kernel(padded, mine_ref, theirs_ref, *refs):
    weights, own_ref, send_ref = refs[:-2], refs[-2], refs[-1]
    for e in range(len(weights) // 3):
        gate_ref, up_ref, down_ref = weights[3 * e : 3 * e + 3]
        at = slice(e * padded, (e + 1) * padded)
        rows = jnp.concatenate([mine_ref[at, :], theirs_ref[at, :]], axis=0)
        gate = dot_nt(rows, gate_ref[...])
        up = dot_nt(rows, up_ref[...])
        hidden = (gate / (1.0 + jnp.exp(-gate)) * up).astype(jnp.bfloat16)
        part = dot(hidden, down_ref[...])
        own_ref[at, :] = part[:padded, :]
        send_ref[at, :] = part[padded:, :].astype(jnp.bfloat16)


def combine_kernel(block, route_ref, *refs):
    groups = len(refs) - 2
    ins, out_ref, held = refs[:groups], refs[groups], refs[groups + 1]
    for g in range(groups):
        held[g * block : (g + 1) * block, :] = ins[g][...]
    rows = route_ref.shape[0]
    place = iota((rows, groups * block), 1)
    slots = [route_ref[:, k : k + 1].astype(jnp.int32) for k in range(TOPK)]
    gates = [route_ref[:, TOPK + k : TOPK + k + 1] for k in range(TOPK)]
    picks = [(place == s).astype(jnp.bfloat16) for s in slots]
    step = 512
    for c in range(0, out_ref.shape[1], step):
        part = held[:, c : c + step]
        total = sum(gates[k] * dot(picks[k], part) for k in range(TOPK))
        out_ref[:, c : c + step] = total.astype(jnp.bfloat16)


def params(limit):
    return pltpu.CompilerParams(vmem_limit_bytes=limit * MIB)


def cost(flops, moved):
    return pl.CostEstimate(flops=flops, bytes_accessed=moved, transcendentals=0)


def whole(count):
    return [pl.BlockSpec(memory_space=VMEM)] * count


def fast(tokens, route_ids, route_gates, gate_weight, up_weight, down_weight):
    rows, width = tokens.shape
    groups = lax.axis_size("expert")
    local_experts, _, half = gate_weight.shape
    block = local_experts * CAP
    bf16 = jnp.bfloat16
    place = jnp.stack([lax.axis_index("expert"), lax.axis_index("dp")]).astype(jnp.int32)
    smem = pl.BlockSpec(memory_space=pltpu.SMEM)
    hbm = pl.BlockSpec(memory_space=pltpu.HBM)
    gate_rows = pltpu.with_memory_space_constraint(jnp.swapaxes(gate_weight, 1, 2), pltpu.HBM)
    up_rows = pltpu.with_memory_space_constraint(jnp.swapaxes(up_weight, 1, 2), pltpu.HBM)
    down_weight = pltpu.with_memory_space_constraint(down_weight, pltpu.HBM)

    packed = pl.pallas_call(
        functools.partial(pack_kernel, local_experts, groups),
        out_shape=[jax.ShapeDtypeStruct((rows, rows), jnp.float32)]
        + [jax.ShapeDtypeStruct((block, width), bf16)] * groups,
        in_specs=[smem] + whole(3),
        out_specs=whole(1 + groups),
        compiler_params=params(4),
        cost_estimate=cost(2 * groups * block * rows * width, 2 * 3 * rows * width),
        name="pack",
    )(place, route_ids.T, route_gates.T, tokens)
    route, outgoing = packed[0], packed[1:]

    def hop(x, k):
        return lax.ppermute(x, "expert", [(i, i ^ k) for i in range(groups)])

    def swap(x):
        return lax.ppermute(x, "dp", [(0, 1), (1, 0)])

    order = [1, 2, 3, 4, 5, 6, 7]
    incoming = {0: outgoing[0]}
    for k in order:
        held = outgoing[k]
        if k > 5:
            held, _ = lax.optimization_barrier((held, incoming[1]))
        incoming[k] = hop(held, k)
    route_now, _, _ = lax.optimization_barrier((route, incoming[1], incoming[2]))

    share = jax.ShapeDtypeStruct((half, width), bf16)
    pieces = 3 * local_experts
    weights = pl.pallas_call(
        functools.partial(load_kernel, half),
        out_shape=[share] * pieces,
        in_specs=[smem] + whole(1) + [hbm] * 3,
        out_specs=whole(pieces),
        scratch_shapes=[pltpu.SemaphoreType.DMA((pieces,))],
        compiler_params=params(1),
        cost_estimate=cost(0, 6 * local_experts * half * width),
        name="load",
    )(place, route_now, gate_rows, up_rows, down_weight)
    incoming[4], gate_now = lax.optimization_barrier((incoming[4], weights[0]))
    weights = [gate_now] + list(weights[1:])

    tall = groups * CAP * local_experts
    half_rows = jax.ShapeDtypeStruct((tall // 2, width), bf16)
    mine = pl.pallas_call(
        functools.partial(regroup_kernel, local_experts, groups),
        out_shape=[half_rows] * 2,
        in_specs=whole(groups),
        out_specs=whole(2),
        scratch_shapes=[VMEM((groups * block, width), bf16)],
        compiler_params=params(4),
        cost_estimate=cost(2 * tall * groups * block * width, 4 * tall * width),
        name="regroup",
    )(*[incoming[k] for k in range(groups)])
    own, other = [], []
    for h in range(2):
        theirs = swap(mine[h])
        kept, send = pl.pallas_call(
            functools.partial(ffn_kernel, groups * CAP),
            out_shape=[jax.ShapeDtypeStruct((tall // 2, width), jnp.float32), half_rows],
            in_specs=whole(2 + pieces // 2),
            out_specs=whole(2),
            compiler_params=params(8),
            cost_estimate=cost(6 * tall * width * half, 3 * local_experts * half * width),
            name="ffn",
        )(mine[h], theirs, *weights[h * pieces // 2 : (h + 1) * pieces // 2])
        own.append(kept)
        other.append(swap(send))
    blocks = pl.pallas_call(
        functools.partial(ungroup_kernel, local_experts, groups),
        out_shape=[jax.ShapeDtypeStruct((block, width), bf16)] * groups,
        in_specs=whole(4),
        out_specs=whole(groups),
        compiler_params=params(4),
        cost_estimate=cost(2 * tall * groups * block * width, 4 * tall * width),
        name="ungroup",
    )(*own, *other)
    returned = {k: hop(blocks[k], k) if k else blocks[k] for k in [0] + order}

    return pl.pallas_call(
        functools.partial(combine_kernel, block),
        out_shape=jax.ShapeDtypeStruct((rows, width), bf16),
        in_specs=whole(1 + groups),
        out_specs=whole(1)[0],
        scratch_shapes=[VMEM((groups * block, width), bf16)],
        compiler_params=params(4),
        cost_estimate=cost(4 * rows * groups * block * width, 4 * rows * width),
        name="combine",
    )(route, *[returned[k] for k in range(groups)])


def on_device(tokens, route_ids, route_gates, gate_weight, up_weight, down_weight):
    suits = (
        lax.axis_size("expert") == 8
        and lax.axis_size("dp") == 2
        and down_weight.shape[1] == FF
        and gate_weight.shape[0] == 4
        and tokens.shape[0] == 128
    )
    run = fast if suits else general
    return run(tokens, route_ids, route_gates, gate_weight, up_weight, down_weight)


def solution(mesh):
    placed = (
        P(("parts", "expert", "dp"), None),
        P(("parts", "expert", "dp"), None),
        P(("parts", "expert", "dp"), None),
        P("expert", None, "dp"),
        P("expert", None, "dp"),
        P("expert", None, None),
    )
    return jax.shard_map(
        on_device,
        mesh=mesh,
        in_specs=placed,
        out_specs=P(("parts", "expert", "dp"), None),
        check_vma=False,
    )
```

```python
import functools

import jax
import jax.numpy as jnp
from jax import lax
from jax.experimental import pallas as pl
from jax.experimental.pallas import tpu as pltpu
from jax.sharding import PartitionSpec as P

FF = 1408
EXPERTS = 32
CAP = 10
TOPK = 2


def general(tokens, route_ids, route_gates, gate_weight, up_weight, down_weight):
    row_count = tokens.shape[0]
    width = tokens.shape[1]
    local_segs = gate_weight.shape[0]
    seg_width = down_weight.shape[1]
    groups = lax.axis_size("expert")
    per_expert = FF // seg_width
    expert_iota = jnp.arange(EXPERTS, dtype=jnp.int32)
    matched = route_ids[:, :, None] == expert_iota[None, None, :]
    member = jnp.sum(matched.astype(jnp.int32), axis=1)
    weighting = jnp.sum(jnp.where(matched, route_gates[:, :, None], jnp.float32(0.0)), axis=1)
    ranking = jnp.cumsum(member, axis=0) - member
    slot_iota = jnp.arange(CAP, dtype=jnp.int32)
    placed = (member[:, :, None] == 1) & (ranking[:, :, None] == slot_iota[None, None, :])
    placed_flat = placed.reshape(row_count, EXPERTS * CAP)
    chooser = placed_flat.astype(jnp.bfloat16)
    packed = jnp.dot(chooser.T, tokens, preferred_element_type=jnp.float32).astype(jnp.bfloat16)
    packed_four = packed.reshape(EXPERTS, 1, CAP, width)
    outgoing = jnp.broadcast_to(packed_four, (EXPERTS, per_expert, CAP, width))
    outgoing = outgoing.reshape(groups, local_segs, CAP, width)
    incoming = lax.all_to_all(outgoing, "expert", split_axis=0, concat_axis=0, tiled=True)
    full_gate, full_up = (
        lax.all_gather(gate_weight, "dp", axis=2, tiled=True),
        lax.all_gather(up_weight, "dp", axis=2, tiled=True),
    )
    gate_val = jnp.einsum("gscd,sdf->gscf", incoming, full_gate, preferred_element_type=jnp.float32)
    up_val = jnp.einsum("gscd,sdf->gscf", incoming, full_up, preferred_element_type=jnp.float32)
    hidden = (jax.nn.silu(gate_val) * up_val).astype(jnp.bfloat16)
    partial_value = jnp.einsum(
        "gscf,sfd->gscd", hidden, down_weight, preferred_element_type=jnp.float32
    ).astype(jnp.bfloat16)
    returned = lax.all_to_all(partial_value, "expert", split_axis=0, concat_axis=0, tiled=True)
    per_seg = returned.reshape(EXPERTS, per_expert, CAP, width).astype(jnp.float32)
    expert_out = jnp.sum(per_seg, axis=1).reshape(EXPERTS * CAP, width)
    combine = jnp.where(placed, weighting[:, :, None], jnp.float32(0.0)).reshape(
        row_count, EXPERTS * CAP
    )
    output = jnp.dot(
        combine, expert_out, precision=lax.Precision.HIGHEST, preferred_element_type=jnp.float32
    )
    return output.astype(jnp.bfloat16)


VMEM = pltpu.VMEM
MIB = 1 << 20


def dot(a, b):
    return jnp.dot(a, b, preferred_element_type=jnp.float32)


def dot_nt(a, b):
    return lax.dot_general(a, b, (((1,), (1,)), ((), ())), preferred_element_type=jnp.float32)


def iota(shape, axis):
    return lax.broadcasted_iota(jnp.int32, shape, axis)


def pack_kernel(local_experts, groups, place_ref, ids_hbm, gates_hbm, tokens_hbm, *outs):
    route_ref, blocks = outs[0], outs[1 : 1 + groups]
    ids_ref, gates_ref, tokens_ref, sems = outs[1 + groups :]
    copies = [
        pltpu.make_async_copy(source, target, sems.at[at])
        for at, (source, target) in enumerate(
            ((ids_hbm, ids_ref), (gates_hbm, gates_ref), (tokens_hbm, tokens_ref))
        )
    ]
    for copy in copies:
        copy.start()
    copies[0].wait()
    rows = tokens_ref.shape[0]
    block = local_experts * CAP
    me = place_ref[0]
    ids = ids_ref[...]
    expert = iota((EXPERTS, rows), 0)
    picks = [(expert == ids[k : k + 1, :]).astype(jnp.float32) for k in range(TOPK)]
    member = functools.reduce(lambda a, b: a + b, picks)
    earlier = (iota((rows, rows), 0) < iota((rows, rows), 1)).astype(jnp.bfloat16)
    ranking = dot(member.astype(jnp.bfloat16), earlier)
    shift = local_experts.bit_length() - 1
    slots = []
    for k in range(TOPK):
        rank = jnp.sum(picks[k] * ranking, axis=0, keepdims=True).astype(jnp.int32)
        one = ids[k : k + 1, :]
        slots.append(((one >> shift) ^ me) * block + (one & (local_experts - 1)) * CAP + rank)
    place = iota((groups * block, rows), 0)
    chosen = functools.reduce(lambda a, b: a | b, [place == s for s in slots])
    chooser = chosen.astype(jnp.bfloat16)
    copies[1].wait()
    copies[2].wait()
    step = 512
    for c in range(0, tokens_ref.shape[1], step):
        got = dot(chooser, tokens_ref[:, c : c + step]).astype(jnp.bfloat16)
        for g in range(groups):
            blocks[g][:, c : c + step] = got[g * block : (g + 1) * block, :]
    columns = [s.astype(jnp.float32) for s in slots] + [gates_ref[...]]
    columns.append(jnp.zeros((rows - 2 * TOPK, rows), jnp.float32))
    route_ref[...] = jnp.concatenate(columns, axis=0).T


def regroup_kernel(local_experts, count, *refs):
    ins, low_ref, high_ref, held = refs[:count], refs[count], refs[count + 1], refs[count + 2]
    block, each = local_experts * CAP, count * CAP
    for b in range(count):
        held[b * block : (b + 1) * block, :] = ins[b][...]
    q = iota((local_experts * each, 1), 0)
    e = sum((q >= k * each).astype(jnp.int32) for k in range(1, local_experts))
    j = q - e * each
    b = (j * 205) >> 11
    source = b * block + e * CAP + (j - b * CAP)
    mover = (iota((local_experts * each, count * block), 1) == source).astype(jnp.bfloat16)
    step, middle = 512, low_ref.shape[0]
    for c in range(0, held.shape[1], step):
        got = dot(mover, held[:, c : c + step]).astype(jnp.bfloat16)
        low_ref[:, c : c + step] = got[:middle, :]
        high_ref[:, c : c + step] = got[middle:, :]


def ungroup_kernel(local_experts, count, own_low, own_high, other_low, other_high, *refs):
    block, each = local_experts * CAP, count * CAP
    s = iota((count * block, 1), 0)
    b = (s * 1639) >> 16
    t = s - b * block
    e = (t * 205) >> 11
    source = e * each + b * CAP + (t - e * CAP)
    mover = (iota((count * block, local_experts * each), 1) == source).astype(jnp.bfloat16)
    step = 512
    for c in range(0, own_low.shape[1], step):
        at = slice(c, c + step)
        parts = [
            (own[:, at] + other[:, at].astype(jnp.float32)).astype(jnp.bfloat16)
            for own, other in ((own_low, other_low), (own_high, other_high))
        ]
        got = dot(mover, jnp.concatenate(parts, axis=0)).astype(jnp.bfloat16)
        for k in range(count):
            refs[k][:, at] = got[k * block : (k + 1) * block, :]


def load_kernel(half, place_ref, _, gate_hbm, up_hbm, down_hbm, *refs):
    count = 3 * gate_hbm.shape[0]
    outs, staged, sems = refs[:count], refs[count], refs[count + 1]
    depth = staged.shape[0]
    first = pl.multiple_of(place_ref[1] * half, 8)
    turned, plain = [], []
    for e in range(gate_hbm.shape[0]):
        for at, source in ((3 * e, gate_hbm.at[e]), (3 * e + 1, up_hbm.at[e])):
            slot = len(turned) % depth
            turned.append((pltpu.make_async_copy(source, staged.at[slot], sems.at[at]), at, slot))
        source = down_hbm.at[e, pl.ds(first, half), :]
        plain.append(pltpu.make_async_copy(source, outs[3 * e + 2], sems.at[3 * e + 2]))
    for at in range(depth):
        turned[at][0].start()
    for n, (copy, at, slot) in enumerate(turned):
        copy.wait()
        step = 256
        for c in range(0, staged.shape[2], step):
            outs[at][c : c + step, :] = staged[slot, :, c : c + step].T
        if n + depth < len(turned):
            turned[n + depth][0].start()
        if n % 2 == 0:
            plain[n // 2].start()
    for copy in plain:
        copy.wait()


def ffn_kernel(padded, mine_ref, theirs_ref, *refs):
    weights, own_ref, send_ref = refs[:-2], refs[-2], refs[-1]
    for e in range(len(weights) // 3):
        gate_ref, up_ref, down_ref = weights[3 * e : 3 * e + 3]
        at = slice(e * padded, (e + 1) * padded)
        rows = jnp.concatenate([mine_ref[at, :], theirs_ref[at, :]], axis=0)
        gate = dot(rows, gate_ref[...])
        up = dot(rows, up_ref[...])
        hidden = (gate / (1.0 + jnp.exp(-gate)) * up).astype(jnp.bfloat16)
        part = dot(hidden, down_ref[...])
        own_ref[at, :] = part[:padded, :]
        send_ref[at, :] = part[padded:, :].astype(jnp.bfloat16)


def combine_kernel(block, members, first, *refs):
    count = len(members)
    held = refs[-1]
    out_ref = refs[-2]
    route_ref, ins = refs[0], refs[1 : 1 + count]
    for at in range(count):
        held[at * block : (at + 1) * block, :] = ins[at][...]
    rows = route_ref.shape[0]
    lane = iota((rows, count * block), 1)
    place = lane
    for at, k in enumerate(members):
        place = jnp.where((lane >= at * block) & (lane < (at + 1) * block), lane + (k - at) * block, place)
    slots = [route_ref[:, k : k + 1].astype(jnp.int32) for k in range(TOPK)]
    gates = [route_ref[:, TOPK + k : TOPK + k + 1] for k in range(TOPK)]
    picks = [(place == s).astype(jnp.bfloat16) for s in slots]
    step = 512
    for c in range(0, out_ref.shape[1], step):
        part = held[:, c : c + step]
        total = sum(gates[k] * dot(picks[k], part) for k in range(TOPK))
        if not first:
            total = total + refs[1 + count][:, c : c + step]
        out_ref[:, c : c + step] = total.astype(out_ref.dtype)


def params(limit):
    return pltpu.CompilerParams(vmem_limit_bytes=limit * MIB)


def cost(flops, moved):
    return pl.CostEstimate(flops=flops, bytes_accessed=moved, transcendentals=0)


def whole(count):
    return [pl.BlockSpec(memory_space=VMEM)] * count


def fast(tokens, route_ids, route_gates, gate_weight, up_weight, down_weight):
    rows, width = tokens.shape
    groups = lax.axis_size("expert")
    local_experts, _, half = gate_weight.shape
    block = local_experts * CAP
    bf16 = jnp.bfloat16
    place = jnp.stack([lax.axis_index("expert"), lax.axis_index("dp")]).astype(jnp.int32)
    smem = pl.BlockSpec(memory_space=pltpu.SMEM)
    hbm = pl.BlockSpec(memory_space=pltpu.HBM)
    gate_rows = pltpu.with_memory_space_constraint(jnp.swapaxes(gate_weight, 1, 2), pltpu.HBM)
    up_rows = pltpu.with_memory_space_constraint(jnp.swapaxes(up_weight, 1, 2), pltpu.HBM)
    down_weight = pltpu.with_memory_space_constraint(down_weight, pltpu.HBM)

    packed = pl.pallas_call(
        functools.partial(pack_kernel, local_experts, groups),
        out_shape=[jax.ShapeDtypeStruct((rows, rows), jnp.float32)]
        + [jax.ShapeDtypeStruct((block, width), bf16)] * groups,
        in_specs=[smem] + [hbm] * 3,
        out_specs=whole(1 + groups),
        scratch_shapes=[
            VMEM((TOPK, rows), jnp.int32),
            VMEM((TOPK, rows), jnp.float32),
            VMEM((rows, width), bf16),
            pltpu.SemaphoreType.DMA((3,)),
        ],
        compiler_params=params(4),
        cost_estimate=cost(2 * groups * block * rows * width, 2 * 3 * rows * width),
        name="pack",
    )(place, *[pltpu.with_memory_space_constraint(x, pltpu.HBM) for x in (route_ids.T, route_gates.T, tokens)])
    route, outgoing = packed[0], packed[1:]

    def hop(x, k):
        return lax.ppermute(x, "expert", [(i, i ^ k) for i in range(groups)])

    def swap(x):
        return lax.ppermute(x, "dp", [(0, 1), (1, 0)])

    order = [1, 2, 3, 4, 5, 6, 7]
    incoming = {0: outgoing[0]}
    for k in order:
        held = outgoing[k]
        if k > 5:
            held, _ = lax.optimization_barrier((held, incoming[1]))
        incoming[k] = hop(held, k)
    route_now, _, _ = lax.optimization_barrier((route, incoming[1], incoming[2]))

    share = jax.ShapeDtypeStruct((half, width), bf16)
    turned = jax.ShapeDtypeStruct((width, half), bf16)
    pieces = 3 * local_experts
    weights = pl.pallas_call(
        functools.partial(load_kernel, half),
        out_shape=[turned, turned, share] * local_experts,
        in_specs=[smem] + whole(1) + [hbm] * 3,
        out_specs=whole(pieces),
        scratch_shapes=[VMEM((3, half, width), bf16), pltpu.SemaphoreType.DMA((pieces,))],
        compiler_params=params(4 + 3 * 3),
        cost_estimate=cost(0, 6 * local_experts * half * width),
        name="load",
    )(place, route_now, gate_rows, up_rows, down_weight)
    incoming[4], gate_now = lax.optimization_barrier((incoming[4], weights[0]))
    weights = [gate_now] + list(weights[1:])

    tall = groups * CAP * local_experts
    half_rows = jax.ShapeDtypeStruct((tall // 2, width), bf16)
    mine = pl.pallas_call(
        functools.partial(regroup_kernel, local_experts, groups),
        out_shape=[half_rows] * 2,
        in_specs=whole(groups),
        out_specs=whole(2),
        scratch_shapes=[VMEM((groups * block, width), bf16)],
        compiler_params=params(4),
        cost_estimate=cost(2 * tall * groups * block * width, 4 * tall * width),
        name="regroup",
    )(*[incoming[k] for k in range(groups)])
    own, other = [], []
    for h in range(2):
        theirs = swap(mine[h])
        kept, send = pl.pallas_call(
            functools.partial(ffn_kernel, groups * CAP),
            out_shape=[jax.ShapeDtypeStruct((tall // 2, width), jnp.float32), half_rows],
            in_specs=whole(2 + pieces // 2),
            out_specs=whole(2),
            compiler_params=params(8),
            cost_estimate=cost(6 * tall * width * half, 3 * local_experts * half * width),
            name="ffn",
        )(mine[h], theirs, *weights[h * pieces // 2 : (h + 1) * pieces // 2])
        own.append(kept)
        other.append(swap(send))
    blocks = pl.pallas_call(
        functools.partial(ungroup_kernel, local_experts, groups),
        out_shape=[jax.ShapeDtypeStruct((block, width), bf16)] * groups,
        in_specs=whole(4),
        out_specs=whole(groups),
        compiler_params=params(4),
        cost_estimate=cost(2 * tall * groups * block * width, 4 * tall * width),
        name="ungroup",
    )(*own, *other)
    returned = {k: hop(blocks[k], k) if k else blocks[k] for k in [0] + order}

    total = None
    parts = [[0, 1, 2, 3, 4], [5, 6, 7]]
    for chunk in parts:
        first, final = total is None, chunk is parts[-1]
        count = len(chunk)
        total = pl.pallas_call(
            functools.partial(combine_kernel, block, chunk, first),
            out_shape=jax.ShapeDtypeStruct((rows, width), bf16 if final else jnp.float32),
            in_specs=whole(1 + count + (not first)),
            out_specs=whole(1)[0],
            scratch_shapes=[VMEM((count * block, width), bf16)],
            compiler_params=params(4),
            cost_estimate=cost(4 * rows * count * block * width, 4 * rows * width),
            name="combine",
        )(route, *[returned[k] for k in chunk], *([] if first else [total]))
    return total


def on_device(tokens, route_ids, route_gates, gate_weight, up_weight, down_weight):
    suits = (
        lax.axis_size("expert") == 8
        and lax.axis_size("dp") == 2
        and down_weight.shape[1] == FF
        and gate_weight.shape[0] == 4
        and tokens.shape[0] == 128
    )
    run = fast if suits else general
    return run(tokens, route_ids, route_gates, gate_weight, up_weight, down_weight)


def solution(mesh):
    placed = (
        P(("parts", "expert", "dp"), None),
        P(("parts", "expert", "dp"), None),
        P(("parts", "expert", "dp"), None),
        P("expert", None, "dp"),
        P("expert", None, "dp"),
        P("expert", None, None),
    )
    return jax.shard_map(
        on_device,
        mesh=mesh,
        in_specs=placed,
        out_specs=P(("parts", "expert", "dp"), None),
        check_vma=False,
    )
```

```python
import functools

import jax
import jax.numpy as jnp
from jax import lax
from jax.experimental import pallas as pl
from jax.experimental.pallas import tpu as pltpu
from jax.sharding import PartitionSpec as P

FF = 1408
EXPERTS = 32
CAP = 10
TOPK = 2


def general(tokens, route_ids, route_gates, gate_weight, up_weight, down_weight):
    row_count = tokens.shape[0]
    width = tokens.shape[1]
    local_segs = gate_weight.shape[0]
    seg_width = down_weight.shape[1]
    groups = lax.axis_size("expert")
    per_expert = FF // seg_width
    expert_iota = jnp.arange(EXPERTS, dtype=jnp.int32)
    matched = route_ids[:, :, None] == expert_iota[None, None, :]
    member = jnp.sum(matched.astype(jnp.int32), axis=1)
    weighting = jnp.sum(jnp.where(matched, route_gates[:, :, None], jnp.float32(0.0)), axis=1)
    ranking = jnp.cumsum(member, axis=0) - member
    slot_iota = jnp.arange(CAP, dtype=jnp.int32)
    placed = (member[:, :, None] == 1) & (ranking[:, :, None] == slot_iota[None, None, :])
    placed_flat = placed.reshape(row_count, EXPERTS * CAP)
    chooser = placed_flat.astype(jnp.bfloat16)
    packed = jnp.dot(chooser.T, tokens, preferred_element_type=jnp.float32).astype(jnp.bfloat16)
    packed_four = packed.reshape(EXPERTS, 1, CAP, width)
    outgoing = jnp.broadcast_to(packed_four, (EXPERTS, per_expert, CAP, width))
    outgoing = outgoing.reshape(groups, local_segs, CAP, width)
    incoming = lax.all_to_all(outgoing, "expert", split_axis=0, concat_axis=0, tiled=True)
    full_gate, full_up = (
        lax.all_gather(gate_weight, "dp", axis=2, tiled=True),
        lax.all_gather(up_weight, "dp", axis=2, tiled=True),
    )
    gate_val = jnp.einsum("gscd,sdf->gscf", incoming, full_gate, preferred_element_type=jnp.float32)
    up_val = jnp.einsum("gscd,sdf->gscf", incoming, full_up, preferred_element_type=jnp.float32)
    hidden = (jax.nn.silu(gate_val) * up_val).astype(jnp.bfloat16)
    partial_value = jnp.einsum(
        "gscf,sfd->gscd", hidden, down_weight, preferred_element_type=jnp.float32
    ).astype(jnp.bfloat16)
    returned = lax.all_to_all(partial_value, "expert", split_axis=0, concat_axis=0, tiled=True)
    per_seg = returned.reshape(EXPERTS, per_expert, CAP, width).astype(jnp.float32)
    expert_out = jnp.sum(per_seg, axis=1).reshape(EXPERTS * CAP, width)
    combine = jnp.where(placed, weighting[:, :, None], jnp.float32(0.0)).reshape(
        row_count, EXPERTS * CAP
    )
    output = jnp.dot(
        combine, expert_out, precision=lax.Precision.HIGHEST, preferred_element_type=jnp.float32
    )
    return output.astype(jnp.bfloat16)


VMEM = pltpu.VMEM
MIB = 1 << 20


def dot(a, b):
    return jnp.dot(a, b, preferred_element_type=jnp.float32)


def dot_nt(a, b):
    return lax.dot_general(a, b, (((1,), (1,)), ((), ())), preferred_element_type=jnp.float32)


def iota(shape, axis):
    return lax.broadcasted_iota(jnp.int32, shape, axis)


def pack_kernel(local_experts, groups, place_ref, ids_hbm, gates_hbm, tokens_hbm, *outs):
    route_ref, blocks = outs[0], outs[1 : 1 + groups]
    ids_ref, gates_ref, tokens_ref, sems = outs[1 + groups :]
    copies = [
        pltpu.make_async_copy(source, target, sems.at[at])
        for at, (source, target) in enumerate(
            ((ids_hbm, ids_ref), (gates_hbm, gates_ref), (tokens_hbm, tokens_ref))
        )
    ]
    for copy in copies:
        copy.start()
    copies[0].wait()
    rows = tokens_ref.shape[0]
    block = local_experts * CAP
    me = place_ref[0]
    ids = ids_ref[...]
    expert = iota((EXPERTS, rows), 0)
    picks = [(expert == ids[k : k + 1, :]).astype(jnp.float32) for k in range(TOPK)]
    member = functools.reduce(lambda a, b: a + b, picks)
    earlier = (iota((rows, rows), 0) < iota((rows, rows), 1)).astype(jnp.bfloat16)
    ranking = dot(member.astype(jnp.bfloat16), earlier)
    shift = local_experts.bit_length() - 1
    slots = []
    for k in range(TOPK):
        rank = jnp.sum(picks[k] * ranking, axis=0, keepdims=True).astype(jnp.int32)
        one = ids[k : k + 1, :]
        slots.append(((one >> shift) ^ me) * block + (one & (local_experts - 1)) * CAP + rank)
    place = iota((groups * block, rows), 0)
    chosen = functools.reduce(lambda a, b: a | b, [place == s for s in slots])
    chooser = chosen.astype(jnp.bfloat16)
    copies[1].wait()
    copies[2].wait()
    step = 512
    for c in range(0, tokens_ref.shape[1], step):
        got = dot(chooser, tokens_ref[:, c : c + step]).astype(jnp.bfloat16)
        for g in range(groups):
            blocks[g][:, c : c + step] = got[g * block : (g + 1) * block, :]
    columns = [s.astype(jnp.float32) for s in slots] + [gates_ref[...]]
    columns.append(jnp.zeros((rows - 2 * TOPK, rows), jnp.float32))
    route_ref[...] = jnp.concatenate(columns, axis=0).T


def regroup_kernel(local_experts, count, *refs):
    ins, low_ref, high_ref, held = refs[:count], refs[count], refs[count + 1], refs[count + 2]
    block, each = local_experts * CAP, count * CAP
    for b in range(count):
        held[b * block : (b + 1) * block, :] = ins[b][...]
    q = iota((local_experts * each, 1), 0)
    e = sum((q >= k * each).astype(jnp.int32) for k in range(1, local_experts))
    j = q - e * each
    b = (j * 205) >> 11
    source = b * block + e * CAP + (j - b * CAP)
    mover = (iota((local_experts * each, count * block), 1) == source).astype(jnp.bfloat16)
    step, middle = 512, low_ref.shape[0]
    for c in range(0, held.shape[1], step):
        got = dot(mover, held[:, c : c + step]).astype(jnp.bfloat16)
        low_ref[:, c : c + step] = got[:middle, :]
        high_ref[:, c : c + step] = got[middle:, :]


def ungroup_kernel(local_experts, count, own_low, own_high, other_low, other_high, *refs):
    block, each = local_experts * CAP, count * CAP
    s = iota((count * block, 1), 0)
    b = (s * 1639) >> 16
    t = s - b * block
    e = (t * 205) >> 11
    source = e * each + b * CAP + (t - e * CAP)
    mover = (iota((count * block, local_experts * each), 1) == source).astype(jnp.bfloat16)
    step = 512
    for c in range(0, own_low.shape[1], step):
        at = slice(c, c + step)
        parts = [
            (own[:, at] + other[:, at].astype(jnp.float32)).astype(jnp.bfloat16)
            for own, other in ((own_low, other_low), (own_high, other_high))
        ]
        got = dot(mover, jnp.concatenate(parts, axis=0)).astype(jnp.bfloat16)
        for k in range(count):
            refs[k][:, at] = got[k * block : (k + 1) * block, :]


def load_kernel(half, place_ref, _, gate_hbm, up_hbm, down_hbm, *refs):
    count = 3 * gate_hbm.shape[0]
    outs, staged, sems = refs[:count], refs[count], refs[count + 1]
    depth = staged.shape[0]
    first = pl.multiple_of(place_ref[1] * half, 8)
    turned, plain = [], []
    for e in range(gate_hbm.shape[0]):
        for at, source in ((3 * e, gate_hbm.at[e]), (3 * e + 1, up_hbm.at[e])):
            slot = len(turned) % depth
            turned.append((pltpu.make_async_copy(source, staged.at[slot], sems.at[at]), at, slot))
        source = down_hbm.at[e, pl.ds(first, half), :]
        plain.append(pltpu.make_async_copy(source, outs[3 * e + 2], sems.at[3 * e + 2]))
    for at in range(depth):
        turned[at][0].start()
    for n, (copy, at, slot) in enumerate(turned):
        copy.wait()
        step = 256
        for c in range(0, staged.shape[2], step):
            outs[at][c : c + step, :] = staged[slot, :, c : c + step].T
        if n + depth < len(turned):
            turned[n + depth][0].start()
        if n % 2 == 0:
            plain[n // 2].start()
    for copy in plain:
        copy.wait()


def ffn_kernel(padded, mine_ref, theirs_ref, *refs):
    weights, own_ref, send_ref = refs[:-2], refs[-2], refs[-1]
    for e in range(len(weights) // 3):
        gate_ref, up_ref, down_ref = weights[3 * e : 3 * e + 3]
        at = slice(e * padded, (e + 1) * padded)
        rows = jnp.concatenate([mine_ref[at, :], theirs_ref[at, :]], axis=0)
        gate = dot(rows, gate_ref[...])
        up = dot(rows, up_ref[...])
        hidden = (gate / (1.0 + jnp.exp(-gate)) * up).astype(jnp.bfloat16)
        part = dot(hidden, down_ref[...])
        own_ref[at, :] = part[:padded, :]
        send_ref[at, :] = part[padded:, :].astype(jnp.bfloat16)


def combine_kernel(block, members, first, *refs):
    count = len(members)
    held = refs[-1]
    out_ref = refs[-2]
    route_ref, ins = refs[0], refs[1 : 1 + count]
    for at in range(count):
        held[at * block : (at + 1) * block, :] = ins[at][...]
    rows = route_ref.shape[0]
    lane = iota((rows, count * block), 1)
    place = lane
    for at, k in enumerate(members):
        place = jnp.where((lane >= at * block) & (lane < (at + 1) * block), lane + (k - at) * block, place)
    slots = [route_ref[:, k : k + 1].astype(jnp.int32) for k in range(TOPK)]
    gates = [route_ref[:, TOPK + k : TOPK + k + 1] for k in range(TOPK)]
    picks = [(place == s).astype(jnp.bfloat16) for s in slots]
    step = 512
    for c in range(0, out_ref.shape[1], step):
        part = held[:, c : c + step]
        total = sum(gates[k] * dot(picks[k], part) for k in range(TOPK))
        if not first:
            total = total + refs[1 + count][:, c : c + step]
        out_ref[:, c : c + step] = total.astype(out_ref.dtype)


def params(limit):
    return pltpu.CompilerParams(vmem_limit_bytes=limit * MIB)


def cost(flops, moved):
    return pl.CostEstimate(flops=flops, bytes_accessed=moved, transcendentals=0)


def whole(count):
    return [pl.BlockSpec(memory_space=VMEM)] * count


def fast(tokens, route_ids, route_gates, gate_weight, up_weight, down_weight):
    rows, width = tokens.shape
    groups = lax.axis_size("expert")
    local_experts, _, half = gate_weight.shape
    block = local_experts * CAP
    bf16 = jnp.bfloat16
    place = jnp.stack([lax.axis_index("expert"), lax.axis_index("dp")]).astype(jnp.int32)
    smem = pl.BlockSpec(memory_space=pltpu.SMEM)
    hbm = pl.BlockSpec(memory_space=pltpu.HBM)
    gate_rows = pltpu.with_memory_space_constraint(jnp.swapaxes(gate_weight, 1, 2), pltpu.HBM)
    up_rows = pltpu.with_memory_space_constraint(jnp.swapaxes(up_weight, 1, 2), pltpu.HBM)
    down_weight = pltpu.with_memory_space_constraint(down_weight, pltpu.HBM)

    packed = pl.pallas_call(
        functools.partial(pack_kernel, local_experts, groups),
        out_shape=[jax.ShapeDtypeStruct((rows, rows), jnp.float32)]
        + [jax.ShapeDtypeStruct((block, width), bf16)] * groups,
        in_specs=[smem] + [hbm] * 3,
        out_specs=whole(1 + groups),
        scratch_shapes=[
            VMEM((TOPK, rows), jnp.int32),
            VMEM((TOPK, rows), jnp.float32),
            VMEM((rows, width), bf16),
            pltpu.SemaphoreType.DMA((3,)),
        ],
        compiler_params=params(4),
        cost_estimate=cost(2 * groups * block * rows * width, 2 * 3 * rows * width),
        name="pack",
    )(place, *[pltpu.with_memory_space_constraint(x, pltpu.HBM) for x in (route_ids.T, route_gates.T, tokens)])
    route, outgoing = packed[0], packed[1:]

    def hop(x, k):
        return lax.ppermute(x, "expert", [(i, i ^ k) for i in range(groups)])

    def swap(x):
        return lax.ppermute(x, "dp", [(0, 1), (1, 0)])

    order = [1, 2, 4, 5, 6, 3, 7]
    incoming = {0: outgoing[0]}
    for k in order:
        held = outgoing[k]
        if k in (3, 7):
            held, _ = lax.optimization_barrier((held, incoming[1]))
        incoming[k] = hop(held, k)
    route_now, _, _ = lax.optimization_barrier((route, incoming[1], incoming[2]))

    share = jax.ShapeDtypeStruct((half, width), bf16)
    turned = jax.ShapeDtypeStruct((width, half), bf16)
    pieces = 3 * local_experts
    weights = pl.pallas_call(
        functools.partial(load_kernel, half),
        out_shape=[turned, turned, share] * local_experts,
        in_specs=[smem] + whole(1) + [hbm] * 3,
        out_specs=whole(pieces),
        scratch_shapes=[VMEM((3, half, width), bf16), pltpu.SemaphoreType.DMA((pieces,))],
        compiler_params=params(4 + 3 * 3),
        cost_estimate=cost(0, 6 * local_experts * half * width),
        name="load",
    )(place, route_now, gate_rows, up_rows, down_weight)
    incoming[4], gate_now = lax.optimization_barrier((incoming[4], weights[0]))
    weights = [gate_now] + list(weights[1:])

    tall = groups * CAP * local_experts
    half_rows = jax.ShapeDtypeStruct((tall // 2, width), bf16)
    mine = pl.pallas_call(
        functools.partial(regroup_kernel, local_experts, groups),
        out_shape=[half_rows] * 2,
        in_specs=whole(groups),
        out_specs=whole(2),
        scratch_shapes=[VMEM((groups * block, width), bf16)],
        compiler_params=params(4),
        cost_estimate=cost(2 * tall * groups * block * width, 4 * tall * width),
        name="regroup",
    )(*[incoming[k] for k in range(groups)])
    own, other = [], []
    for h in range(2):
        theirs = swap(mine[h])
        kept, send = pl.pallas_call(
            functools.partial(ffn_kernel, groups * CAP),
            out_shape=[jax.ShapeDtypeStruct((tall // 2, width), jnp.float32), half_rows],
            in_specs=whole(2 + pieces // 2),
            out_specs=whole(2),
            compiler_params=params(8),
            cost_estimate=cost(6 * tall * width * half, 3 * local_experts * half * width),
            name="ffn",
        )(mine[h], theirs, *weights[h * pieces // 2 : (h + 1) * pieces // 2])
        own.append(kept)
        other.append(swap(send))
    blocks = pl.pallas_call(
        functools.partial(ungroup_kernel, local_experts, groups),
        out_shape=[jax.ShapeDtypeStruct((block, width), bf16)] * groups,
        in_specs=whole(4),
        out_specs=whole(groups),
        compiler_params=params(4),
        cost_estimate=cost(2 * tall * groups * block * width, 4 * tall * width),
        name="ungroup",
    )(*own, *other)
    returned = {k: hop(blocks[k], k) if k else blocks[k] for k in [0] + order}

    total = None
    parts = [[0, 1, 6, 7], [2, 3, 4, 5]]
    for chunk in parts:
        first, final = total is None, chunk is parts[-1]
        count = len(chunk)
        total = pl.pallas_call(
            functools.partial(combine_kernel, block, chunk, first),
            out_shape=jax.ShapeDtypeStruct((rows, width), bf16 if final else jnp.float32),
            in_specs=whole(1 + count + (not first)),
            out_specs=whole(1)[0],
            scratch_shapes=[VMEM((count * block, width), bf16)],
            compiler_params=params(4),
            cost_estimate=cost(4 * rows * count * block * width, 4 * rows * width),
            name="combine",
        )(route, *[returned[k] for k in chunk], *([] if first else [total]))
    return total


def on_device(tokens, route_ids, route_gates, gate_weight, up_weight, down_weight):
    suits = (
        lax.axis_size("expert") == 8
        and lax.axis_size("dp") == 2
        and down_weight.shape[1] == FF
        and gate_weight.shape[0] == 4
        and tokens.shape[0] == 128
    )
    run = fast if suits else general
    return run(tokens, route_ids, route_gates, gate_weight, up_weight, down_weight)


def solution(mesh):
    placed = (
        P(("parts", "expert", "dp"), None),
        P(("parts", "expert", "dp"), None),
        P(("parts", "expert", "dp"), None),
        P("expert", None, "dp"),
        P("expert", None, "dp"),
        P("expert", None, None),
    )
    return jax.shard_map(
        on_device,
        mesh=mesh,
        in_specs=placed,
        out_specs=P(("parts", "expert", "dp"), None),
        check_vma=False,
    )
```

```python
import functools

import jax
import jax.numpy as jnp
from jax import lax
from jax.experimental import pallas as pl
from jax.experimental.pallas import tpu as pltpu
from jax.sharding import PartitionSpec as P

FF = 1408
EXPERTS = 32
CAP = 10
TOPK = 2


def general(tokens, route_ids, route_gates, gate_weight, up_weight, down_weight):
    row_count = tokens.shape[0]
    width = tokens.shape[1]
    local_segs = gate_weight.shape[0]
    seg_width = down_weight.shape[1]
    groups = lax.axis_size("expert")
    per_expert = FF // seg_width
    expert_iota = jnp.arange(EXPERTS, dtype=jnp.int32)
    matched = route_ids[:, :, None] == expert_iota[None, None, :]
    member = jnp.sum(matched.astype(jnp.int32), axis=1)
    weighting = jnp.sum(jnp.where(matched, route_gates[:, :, None], jnp.float32(0.0)), axis=1)
    ranking = jnp.cumsum(member, axis=0) - member
    slot_iota = jnp.arange(CAP, dtype=jnp.int32)
    placed = (member[:, :, None] == 1) & (ranking[:, :, None] == slot_iota[None, None, :])
    placed_flat = placed.reshape(row_count, EXPERTS * CAP)
    chooser = placed_flat.astype(jnp.bfloat16)
    packed = jnp.dot(chooser.T, tokens, preferred_element_type=jnp.float32).astype(jnp.bfloat16)
    packed_four = packed.reshape(EXPERTS, 1, CAP, width)
    outgoing = jnp.broadcast_to(packed_four, (EXPERTS, per_expert, CAP, width))
    outgoing = outgoing.reshape(groups, local_segs, CAP, width)
    incoming = lax.all_to_all(outgoing, "expert", split_axis=0, concat_axis=0, tiled=True)
    full_gate, full_up = (
        lax.all_gather(gate_weight, "dp", axis=2, tiled=True),
        lax.all_gather(up_weight, "dp", axis=2, tiled=True),
    )
    gate_val = jnp.einsum("gscd,sdf->gscf", incoming, full_gate, preferred_element_type=jnp.float32)
    up_val = jnp.einsum("gscd,sdf->gscf", incoming, full_up, preferred_element_type=jnp.float32)
    hidden = (jax.nn.silu(gate_val) * up_val).astype(jnp.bfloat16)
    partial_value = jnp.einsum(
        "gscf,sfd->gscd", hidden, down_weight, preferred_element_type=jnp.float32
    ).astype(jnp.bfloat16)
    returned = lax.all_to_all(partial_value, "expert", split_axis=0, concat_axis=0, tiled=True)
    per_seg = returned.reshape(EXPERTS, per_expert, CAP, width).astype(jnp.float32)
    expert_out = jnp.sum(per_seg, axis=1).reshape(EXPERTS * CAP, width)
    combine = jnp.where(placed, weighting[:, :, None], jnp.float32(0.0)).reshape(
        row_count, EXPERTS * CAP
    )
    output = jnp.dot(
        combine, expert_out, precision=lax.Precision.HIGHEST, preferred_element_type=jnp.float32
    )
    return output.astype(jnp.bfloat16)


VMEM = pltpu.VMEM
MIB = 1 << 20


def dot(a, b):
    return jnp.dot(a, b, preferred_element_type=jnp.float32)


def dot_nt(a, b):
    return lax.dot_general(a, b, (((1,), (1,)), ((), ())), preferred_element_type=jnp.float32)


def iota(shape, axis):
    return lax.broadcasted_iota(jnp.int32, shape, axis)


def pack_kernel(local_experts, groups, place_ref, ids_hbm, gates_hbm, tokens_hbm, *outs):
    route_ref, blocks = outs[0], outs[1 : 1 + groups]
    ids_ref, gates_ref, tokens_ref, sems = outs[1 + groups :]
    copies = [
        pltpu.make_async_copy(source, target, sems.at[at])
        for at, (source, target) in enumerate(
            ((ids_hbm, ids_ref), (gates_hbm, gates_ref), (tokens_hbm, tokens_ref))
        )
    ]
    for copy in copies:
        copy.start()
    copies[0].wait()
    rows = tokens_ref.shape[0]
    block = local_experts * CAP
    me = place_ref[0]
    ids = ids_ref[...]
    expert = iota((EXPERTS, rows), 0)
    picks = [(expert == ids[k : k + 1, :]).astype(jnp.float32) for k in range(TOPK)]
    member = functools.reduce(lambda a, b: a + b, picks)
    earlier = (iota((rows, rows), 0) < iota((rows, rows), 1)).astype(jnp.bfloat16)
    ranking = dot(member.astype(jnp.bfloat16), earlier)
    shift = local_experts.bit_length() - 1
    slots = []
    for k in range(TOPK):
        rank = jnp.sum(picks[k] * ranking, axis=0, keepdims=True).astype(jnp.int32)
        one = ids[k : k + 1, :]
        slots.append(((one >> shift) ^ me) * block + (one & (local_experts - 1)) * CAP + rank)
    place = iota((groups * block, rows), 0)
    chosen = functools.reduce(lambda a, b: a | b, [place == s for s in slots])
    chooser = chosen.astype(jnp.bfloat16)
    copies[1].wait()
    copies[2].wait()
    step = 512
    for c in range(0, tokens_ref.shape[1], step):
        got = dot(chooser, tokens_ref[:, c : c + step]).astype(jnp.bfloat16)
        for g in range(groups):
            blocks[g][:, c : c + step] = got[g * block : (g + 1) * block, :]
    columns = [s.astype(jnp.float32) for s in slots] + [gates_ref[...]]
    columns.append(jnp.zeros((8 - 2 * TOPK, rows), jnp.float32))
    route_ref[...] = jnp.concatenate(columns, axis=0)


def regroup_kernel(local_experts, count, *refs):
    ins, low_ref, high_ref, held = refs[:count], refs[count], refs[count + 1], refs[count + 2]
    block, each = local_experts * CAP, count * CAP
    for b in range(count):
        held[b * block : (b + 1) * block, :] = ins[b][...]
    q = iota((local_experts * each, 1), 0)
    e = sum((q >= k * each).astype(jnp.int32) for k in range(1, local_experts))
    j = q - e * each
    b = (j * 205) >> 11
    source = b * block + e * CAP + (j - b * CAP)
    mover = (iota((local_experts * each, count * block), 1) == source).astype(jnp.bfloat16)
    step, middle = 512, low_ref.shape[0]
    for c in range(0, held.shape[1], step):
        got = dot(mover, held[:, c : c + step]).astype(jnp.bfloat16)
        low_ref[:, c : c + step] = got[:middle, :]
        high_ref[:, c : c + step] = got[middle:, :]


def ungroup_kernel(local_experts, count, own_low, own_high, other_low, other_high, *refs):
    block, each = local_experts * CAP, count * CAP
    s = iota((count * block, 1), 0)
    b = (s * 1639) >> 16
    t = s - b * block
    e = (t * 205) >> 11
    source = e * each + b * CAP + (t - e * CAP)
    mover = (iota((count * block, local_experts * each), 1) == source).astype(jnp.bfloat16)
    step = 512
    for c in range(0, own_low.shape[1], step):
        at = slice(c, c + step)
        parts = [
            (own[:, at] + other[:, at].astype(jnp.float32)).astype(jnp.bfloat16)
            for own, other in ((own_low, other_low), (own_high, other_high))
        ]
        got = dot(mover, jnp.concatenate(parts, axis=0)).astype(jnp.bfloat16)
        for k in range(count):
            refs[k][:, at] = got[k * block : (k + 1) * block, :]


def load_kernel(half, place_ref, route_ref, gate_hbm, up_hbm, down_hbm, *refs):
    count = 3 * gate_hbm.shape[0]
    outs, columns_ref, staged, sems = refs[:count], refs[count], refs[count + 1], refs[count + 2]
    depth = staged.shape[0]
    first = pl.multiple_of(place_ref[1] * half, 8)
    turned, plain = [], []
    for e in range(gate_hbm.shape[0]):
        for at, source in ((3 * e, gate_hbm.at[e]), (3 * e + 1, up_hbm.at[e])):
            slot = len(turned) % depth
            turned.append((pltpu.make_async_copy(source, staged.at[slot], sems.at[at]), at, slot))
        source = down_hbm.at[e, pl.ds(first, half), :]
        plain.append(pltpu.make_async_copy(source, outs[3 * e + 2], sems.at[3 * e + 2]))
    for at in range(depth):
        turned[at][0].start()
    rows = route_ref.shape[1]
    rest = jnp.zeros((rows - route_ref.shape[0], rows), jnp.float32)
    columns_ref[...] = jnp.concatenate([route_ref[...], rest], axis=0).T
    for n, (copy, at, slot) in enumerate(turned):
        copy.wait()
        step = 256
        for c in range(0, staged.shape[2], step):
            outs[at][c : c + step, :] = staged[slot, :, c : c + step].T
        if n + depth < len(turned):
            turned[n + depth][0].start()
        if n % 2 == 0:
            plain[n // 2].start()
    for copy in plain:
        copy.wait()


def ffn_kernel(padded, mine_ref, theirs_ref, *refs):
    weights, own_ref, send_ref = refs[:-2], refs[-2], refs[-1]
    for e in range(len(weights) // 3):
        gate_ref, up_ref, down_ref = weights[3 * e : 3 * e + 3]
        at = slice(e * padded, (e + 1) * padded)
        rows = jnp.concatenate([mine_ref[at, :], theirs_ref[at, :]], axis=0)
        gate = dot(rows, gate_ref[...])
        up = dot(rows, up_ref[...])
        hidden = (gate / (1.0 + jnp.exp(-gate)) * up).astype(jnp.bfloat16)
        part = dot(hidden, down_ref[...])
        own_ref[at, :] = part[:padded, :]
        send_ref[at, :] = part[padded:, :].astype(jnp.bfloat16)


def combine_kernel(block, members, first, *refs):
    count = len(members)
    held = refs[-1]
    out_ref = refs[-2]
    route_ref, ins = refs[0], refs[1 : 1 + count]
    for at in range(count):
        held[at * block : (at + 1) * block, :] = ins[at][...]
    rows = route_ref.shape[0]
    lane = iota((rows, count * block), 1)
    place = lane
    for at, k in enumerate(members):
        place = jnp.where((lane >= at * block) & (lane < (at + 1) * block), lane + (k - at) * block, place)
    slots = [route_ref[:, k : k + 1].astype(jnp.int32) for k in range(TOPK)]
    gates = [route_ref[:, TOPK + k : TOPK + k + 1] for k in range(TOPK)]
    picks = [(place == s).astype(jnp.bfloat16) for s in slots]
    step = 512
    for c in range(0, out_ref.shape[1], step):
        part = held[:, c : c + step]
        total = sum(gates[k] * dot(picks[k], part) for k in range(TOPK))
        if not first:
            total = total + refs[1 + count][:, c : c + step]
        out_ref[:, c : c + step] = total.astype(out_ref.dtype)


def params(limit):
    return pltpu.CompilerParams(vmem_limit_bytes=limit * MIB)


def cost(flops, moved):
    return pl.CostEstimate(flops=flops, bytes_accessed=moved, transcendentals=0)


def whole(count):
    return [pl.BlockSpec(memory_space=VMEM)] * count


def fast(tokens, route_ids, route_gates, gate_weight, up_weight, down_weight):
    rows, width = tokens.shape
    groups = lax.axis_size("expert")
    local_experts, _, half = gate_weight.shape
    block = local_experts * CAP
    bf16 = jnp.bfloat16
    place = jnp.stack([lax.axis_index("expert"), lax.axis_index("dp")]).astype(jnp.int32)
    smem = pl.BlockSpec(memory_space=pltpu.SMEM)
    hbm = pl.BlockSpec(memory_space=pltpu.HBM)
    gate_rows = pltpu.with_memory_space_constraint(jnp.swapaxes(gate_weight, 1, 2), pltpu.HBM)
    up_rows = pltpu.with_memory_space_constraint(jnp.swapaxes(up_weight, 1, 2), pltpu.HBM)
    down_weight = pltpu.with_memory_space_constraint(down_weight, pltpu.HBM)

    packed = pl.pallas_call(
        functools.partial(pack_kernel, local_experts, groups),
        out_shape=[jax.ShapeDtypeStruct((8, rows), jnp.float32)]
        + [jax.ShapeDtypeStruct((block, width), bf16)] * groups,
        in_specs=[smem] + [hbm] * 3,
        out_specs=whole(1 + groups),
        scratch_shapes=[
            VMEM((TOPK, rows), jnp.int32),
            VMEM((TOPK, rows), jnp.float32),
            VMEM((rows, width), bf16),
            pltpu.SemaphoreType.DMA((3,)),
        ],
        compiler_params=params(4),
        cost_estimate=cost(2 * groups * block * rows * width, 2 * 3 * rows * width),
        name="pack",
    )(place, *[pltpu.with_memory_space_constraint(x, pltpu.HBM) for x in (route_ids.T, route_gates.T, tokens)])
    route, outgoing = packed[0], packed[1:]

    def hop(x, k):
        return lax.ppermute(x, "expert", [(i, i ^ k) for i in range(groups)])

    def swap(x):
        return lax.ppermute(x, "dp", [(0, 1), (1, 0)])

    order = [1, 2, 4, 5, 6, 3, 7]
    incoming = {0: outgoing[0]}
    for k in order:
        held = outgoing[k]
        if k in (3, 7):
            held, _ = lax.optimization_barrier((held, incoming[1]))
        incoming[k] = hop(held, k)
    route_now, _, _ = lax.optimization_barrier((route, incoming[1], incoming[2]))

    share = jax.ShapeDtypeStruct((half, width), bf16)
    turned = jax.ShapeDtypeStruct((width, half), bf16)
    pieces = 3 * local_experts
    *weights, columns = pl.pallas_call(
        functools.partial(load_kernel, half),
        out_shape=[turned, turned, share] * local_experts
        + [jax.ShapeDtypeStruct((rows, rows), jnp.float32)],
        in_specs=[smem] + whole(1) + [hbm] * 3,
        out_specs=whole(pieces + 1),
        scratch_shapes=[VMEM((3, half, width), bf16), pltpu.SemaphoreType.DMA((pieces,))],
        compiler_params=params(4 + 3 * 3),
        cost_estimate=cost(0, 6 * local_experts * half * width),
        name="load",
    )(place, route_now, gate_rows, up_rows, down_weight)
    incoming[4], gate_now = lax.optimization_barrier((incoming[4], weights[0]))
    weights = [gate_now] + list(weights[1:])

    tall = groups * CAP * local_experts
    half_rows = jax.ShapeDtypeStruct((tall // 2, width), bf16)
    mine = pl.pallas_call(
        functools.partial(regroup_kernel, local_experts, groups),
        out_shape=[half_rows] * 2,
        in_specs=whole(groups),
        out_specs=whole(2),
        scratch_shapes=[VMEM((groups * block, width), bf16)],
        compiler_params=params(4),
        cost_estimate=cost(2 * tall * groups * block * width, 4 * tall * width),
        name="regroup",
    )(*[incoming[k] for k in range(groups)])
    own, other = [], []
    for h in range(2):
        theirs = swap(mine[h])
        kept, send = pl.pallas_call(
            functools.partial(ffn_kernel, groups * CAP),
            out_shape=[jax.ShapeDtypeStruct((tall // 2, width), jnp.float32), half_rows],
            in_specs=whole(2 + pieces // 2),
            out_specs=whole(2),
            compiler_params=params(8),
            cost_estimate=cost(6 * tall * width * half, 3 * local_experts * half * width),
            name="ffn",
        )(mine[h], theirs, *weights[h * pieces // 2 : (h + 1) * pieces // 2])
        own.append(kept)
        other.append(swap(send))
    blocks = pl.pallas_call(
        functools.partial(ungroup_kernel, local_experts, groups),
        out_shape=[jax.ShapeDtypeStruct((block, width), bf16)] * groups,
        in_specs=whole(4),
        out_specs=whole(groups),
        compiler_params=params(4),
        cost_estimate=cost(2 * tall * groups * block * width, 4 * tall * width),
        name="ungroup",
    )(*own, *other)
    returned = {k: hop(blocks[k], k) if k else blocks[k] for k in [0] + order}

    total = None
    parts = [[0, 1, 6, 7, 2, 3], [4, 5]]
    for chunk in parts:
        first, final = total is None, chunk is parts[-1]
        count = len(chunk)
        total = pl.pallas_call(
            functools.partial(combine_kernel, block, chunk, first),
            out_shape=jax.ShapeDtypeStruct((rows, width), bf16 if final else jnp.float32),
            in_specs=whole(1 + count + (not first)),
            out_specs=whole(1)[0],
            scratch_shapes=[VMEM((count * block, width), bf16)],
            compiler_params=params(4),
            cost_estimate=cost(4 * rows * count * block * width, 4 * rows * width),
            name="combine",
        )(columns, *[returned[k] for k in chunk], *([] if first else [total]))
    return total


def on_device(tokens, route_ids, route_gates, gate_weight, up_weight, down_weight):
    suits = (
        lax.axis_size("expert") == 8
        and lax.axis_size("dp") == 2
        and down_weight.shape[1] == FF
        and gate_weight.shape[0] == 4
        and tokens.shape[0] == 128
    )
    run = fast if suits else general
    return run(tokens, route_ids, route_gates, gate_weight, up_weight, down_weight)


def solution(mesh):
    placed = (
        P(("parts", "expert", "dp"), None),
        P(("parts", "expert", "dp"), None),
        P(("parts", "expert", "dp"), None),
        P("expert", None, "dp"),
        P("expert", None, "dp"),
        P("expert", None, None),
    )
    return jax.shard_map(
        on_device,
        mesh=mesh,
        in_specs=placed,
        out_specs=P(("parts", "expert", "dp"), None),
        check_vma=False,
    )
```

```python
import functools

import jax
import jax.numpy as jnp
from jax import lax
from jax.experimental import pallas as pl
from jax.experimental.pallas import tpu as pltpu
from jax.sharding import PartitionSpec as P

FF = 1408
EXPERTS = 32
CAP = 10
TOPK = 2


def general(tokens, route_ids, route_gates, gate_weight, up_weight, down_weight):
    row_count = tokens.shape[0]
    width = tokens.shape[1]
    local_segs = gate_weight.shape[0]
    seg_width = down_weight.shape[1]
    groups = lax.axis_size("expert")
    per_expert = FF // seg_width
    expert_iota = jnp.arange(EXPERTS, dtype=jnp.int32)
    matched = route_ids[:, :, None] == expert_iota[None, None, :]
    member = jnp.sum(matched.astype(jnp.int32), axis=1)
    weighting = jnp.sum(jnp.where(matched, route_gates[:, :, None], jnp.float32(0.0)), axis=1)
    ranking = jnp.cumsum(member, axis=0) - member
    slot_iota = jnp.arange(CAP, dtype=jnp.int32)
    placed = (member[:, :, None] == 1) & (ranking[:, :, None] == slot_iota[None, None, :])
    placed_flat = placed.reshape(row_count, EXPERTS * CAP)
    chooser = placed_flat.astype(jnp.bfloat16)
    packed = jnp.dot(chooser.T, tokens, preferred_element_type=jnp.float32).astype(jnp.bfloat16)
    packed_four = packed.reshape(EXPERTS, 1, CAP, width)
    outgoing = jnp.broadcast_to(packed_four, (EXPERTS, per_expert, CAP, width))
    outgoing = outgoing.reshape(groups, local_segs, CAP, width)
    incoming = lax.all_to_all(outgoing, "expert", split_axis=0, concat_axis=0, tiled=True)
    full_gate, full_up = (
        lax.all_gather(gate_weight, "dp", axis=2, tiled=True),
        lax.all_gather(up_weight, "dp", axis=2, tiled=True),
    )
    gate_val = jnp.einsum("gscd,sdf->gscf", incoming, full_gate, preferred_element_type=jnp.float32)
    up_val = jnp.einsum("gscd,sdf->gscf", incoming, full_up, preferred_element_type=jnp.float32)
    hidden = (jax.nn.silu(gate_val) * up_val).astype(jnp.bfloat16)
    partial_value = jnp.einsum(
        "gscf,sfd->gscd", hidden, down_weight, preferred_element_type=jnp.float32
    ).astype(jnp.bfloat16)
    returned = lax.all_to_all(partial_value, "expert", split_axis=0, concat_axis=0, tiled=True)
    per_seg = returned.reshape(EXPERTS, per_expert, CAP, width).astype(jnp.float32)
    expert_out = jnp.sum(per_seg, axis=1).reshape(EXPERTS * CAP, width)
    combine = jnp.where(placed, weighting[:, :, None], jnp.float32(0.0)).reshape(
        row_count, EXPERTS * CAP
    )
    output = jnp.dot(
        combine, expert_out, precision=lax.Precision.HIGHEST, preferred_element_type=jnp.float32
    )
    return output.astype(jnp.bfloat16)


VMEM = pltpu.VMEM
MIB = 1 << 20


def dot(a, b):
    return jnp.dot(a, b, preferred_element_type=jnp.float32)


def dot_nt(a, b):
    return lax.dot_general(a, b, (((1,), (1,)), ((), ())), preferred_element_type=jnp.float32)


def iota(shape, axis):
    return lax.broadcasted_iota(jnp.int32, shape, axis)


def pack_kernel(local_experts, groups, place_ref, ids_hbm, gates_hbm, tokens_hbm, *outs):
    route_ref, blocks = outs[0], outs[1 : 1 + groups]
    ids_ref, gates_ref, tokens_ref, sems = outs[1 + groups :]
    copies = [
        pltpu.make_async_copy(source, target, sems.at[at])
        for at, (source, target) in enumerate(
            ((ids_hbm, ids_ref), (gates_hbm, gates_ref), (tokens_hbm, tokens_ref))
        )
    ]
    for copy in copies:
        copy.start()
    copies[0].wait()
    rows = tokens_ref.shape[0]
    block = local_experts * CAP
    me = place_ref[0]
    ids = ids_ref[...]
    expert = iota((EXPERTS, rows), 0)
    picks = [(expert == ids[k : k + 1, :]).astype(jnp.float32) for k in range(TOPK)]
    member = functools.reduce(lambda a, b: a + b, picks)
    earlier = (iota((rows, rows), 0) < iota((rows, rows), 1)).astype(jnp.bfloat16)
    ranking = dot(member.astype(jnp.bfloat16), earlier)
    shift = local_experts.bit_length() - 1
    slots = []
    for k in range(TOPK):
        rank = jnp.sum(picks[k] * ranking, axis=0, keepdims=True).astype(jnp.int32)
        one = ids[k : k + 1, :]
        slots.append(((one >> shift) ^ me) * block + (one & (local_experts - 1)) * CAP + rank)
    place = iota((groups * block, rows), 0)
    chosen = functools.reduce(lambda a, b: a | b, [place == s for s in slots])
    chooser = chosen.astype(jnp.bfloat16)
    copies[1].wait()
    copies[2].wait()
    step = 512
    for c in range(0, tokens_ref.shape[1], step):
        got = dot(chooser, tokens_ref[:, c : c + step]).astype(jnp.bfloat16)
        for g in range(groups):
            blocks[g][:, c : c + step] = got[g * block : (g + 1) * block, :]
    columns = [s.astype(jnp.float32) for s in slots] + [gates_ref[...]]
    columns.append(jnp.zeros((rows - 2 * TOPK, rows), jnp.float32))
    route_ref[...] = jnp.concatenate(columns, axis=0).T


def regroup_kernel(local_experts, count, *refs):
    ins, outs, held = refs[:count], refs[count:-1], refs[-1]
    block, each = local_experts * CAP, count * CAP
    for b in range(count):
        held[b * block : (b + 1) * block, :] = ins[b][...]
    q = iota((local_experts * each, 1), 0)
    e = sum((q >= k * each).astype(jnp.int32) for k in range(1, local_experts))
    j = q - e * each
    b = (j * 205) >> 11
    source = b * block + e * CAP + (j - b * CAP)
    mover = (iota((local_experts * each, count * block), 1) == source).astype(jnp.bfloat16)
    step, tall = 512, outs[0].shape[0]
    for c in range(0, held.shape[1], step):
        got = dot(mover, held[:, c : c + step]).astype(jnp.bfloat16)
        for k, out_ref in enumerate(outs):
            out_ref[:, c : c + step] = got[k * tall : (k + 1) * tall, :]


def ungroup_kernel(local_experts, count, *refs):
    block, each = local_experts * CAP, count * CAP
    kept, refs = refs[:-count], refs[-count:]
    halves = list(zip(kept[: len(kept) // 2], kept[len(kept) // 2 :]))
    s = iota((count * block, 1), 0)
    b = (s * 1639) >> 16
    t = s - b * block
    e = (t * 205) >> 11
    source = e * each + b * CAP + (t - e * CAP)
    mover = (iota((count * block, local_experts * each), 1) == source).astype(jnp.bfloat16)
    step = 512
    for c in range(0, kept[0].shape[1], step):
        at = slice(c, c + step)
        parts = [
            (own[:, at] + other[:, at].astype(jnp.float32)).astype(jnp.bfloat16)
            for own, other in halves
        ]
        got = dot(mover, jnp.concatenate(parts, axis=0)).astype(jnp.bfloat16)
        for k in range(count):
            refs[k][:, at] = got[k * block : (k + 1) * block, :]


def load_kernel(half, place_ref, _, gate_hbm, up_hbm, down_hbm, *refs):
    count = 3 * gate_hbm.shape[0]
    outs, staged, sems = refs[:count], refs[count], refs[count + 1]
    depth = staged.shape[0]
    first = pl.multiple_of(place_ref[1] * half, 8)
    turned, plain = [], []
    for e in range(gate_hbm.shape[0]):
        for at, source in ((3 * e, gate_hbm.at[e]), (3 * e + 1, up_hbm.at[e])):
            slot = len(turned) % depth
            turned.append((pltpu.make_async_copy(source, staged.at[slot], sems.at[at]), at, slot))
        source = down_hbm.at[e, pl.ds(first, half), :]
        plain.append(pltpu.make_async_copy(source, outs[3 * e + 2], sems.at[3 * e + 2]))
    for at in range(depth):
        turned[at][0].start()
    for n, (copy, at, slot) in enumerate(turned):
        copy.wait()
        step = 256
        for c in range(0, staged.shape[2], step):
            outs[at][c : c + step, :] = staged[slot, :, c : c + step].T
        if n + depth < len(turned):
            turned[n + depth][0].start()
        if n % 2 == 0:
            plain[n // 2].start()
    for copy in plain:
        copy.wait()


def ffn_kernel(padded, mine_ref, theirs_ref, *refs):
    weights, own_ref, send_ref = refs[:-2], refs[-2], refs[-1]
    for e in range(len(weights) // 3):
        gate_ref, up_ref, down_ref = weights[3 * e : 3 * e + 3]
        at = slice(e * padded, (e + 1) * padded)
        rows = jnp.concatenate([mine_ref[at, :], theirs_ref[at, :]], axis=0)
        gate = dot(rows, gate_ref[...])
        up = dot(rows, up_ref[...])
        hidden = (gate / (1.0 + jnp.exp(-gate)) * up).astype(jnp.bfloat16)
        part = dot(hidden, down_ref[...])
        own_ref[at, :] = part[:padded, :]
        send_ref[at, :] = part[padded:, :].astype(jnp.bfloat16)


def combine_kernel(block, members, first, *refs):
    count = len(members)
    held = refs[-1]
    out_ref = refs[-2]
    route_ref, ins = refs[0], refs[1 : 1 + count]
    for at in range(count):
        held[at * block : (at + 1) * block, :] = ins[at][...]
    rows = route_ref.shape[0]
    lane = iota((rows, count * block), 1)
    place = lane
    for at, k in enumerate(members):
        place = jnp.where((lane >= at * block) & (lane < (at + 1) * block), lane + (k - at) * block, place)
    slots = [route_ref[:, k : k + 1].astype(jnp.int32) for k in range(TOPK)]
    gates = [route_ref[:, TOPK + k : TOPK + k + 1] for k in range(TOPK)]
    picks = [(place == s).astype(jnp.bfloat16) for s in slots]
    step = 512
    for c in range(0, out_ref.shape[1], step):
        part = held[:, c : c + step]
        total = sum(gates[k] * dot(picks[k], part) for k in range(TOPK))
        if not first:
            total = total + refs[1 + count][:, c : c + step]
        out_ref[:, c : c + step] = total.astype(out_ref.dtype)


def params(limit):
    return pltpu.CompilerParams(vmem_limit_bytes=limit * MIB)


def cost(flops, moved):
    return pl.CostEstimate(flops=flops, bytes_accessed=moved, transcendentals=0)


def whole(count):
    return [pl.BlockSpec(memory_space=VMEM)] * count


def fast(tokens, route_ids, route_gates, gate_weight, up_weight, down_weight):
    rows, width = tokens.shape
    groups = lax.axis_size("expert")
    local_experts, _, half = gate_weight.shape
    block = local_experts * CAP
    bf16 = jnp.bfloat16
    place = jnp.stack([lax.axis_index("expert"), lax.axis_index("dp")]).astype(jnp.int32)
    smem = pl.BlockSpec(memory_space=pltpu.SMEM)
    hbm = pl.BlockSpec(memory_space=pltpu.HBM)
    gate_rows = pltpu.with_memory_space_constraint(jnp.swapaxes(gate_weight, 1, 2), pltpu.HBM)
    up_rows = pltpu.with_memory_space_constraint(jnp.swapaxes(up_weight, 1, 2), pltpu.HBM)
    down_weight = pltpu.with_memory_space_constraint(down_weight, pltpu.HBM)

    packed = pl.pallas_call(
        functools.partial(pack_kernel, local_experts, groups),
        out_shape=[jax.ShapeDtypeStruct((rows, rows), jnp.float32)]
        + [jax.ShapeDtypeStruct((block, width), bf16)] * groups,
        in_specs=[smem] + [hbm] * 3,
        out_specs=whole(1 + groups),
        scratch_shapes=[
            VMEM((TOPK, rows), jnp.int32),
            VMEM((TOPK, rows), jnp.float32),
            VMEM((rows, width), bf16),
            pltpu.SemaphoreType.DMA((3,)),
        ],
        compiler_params=params(4),
        cost_estimate=cost(2 * groups * block * rows * width, 2 * 3 * rows * width),
        name="pack",
    )(place, *[pltpu.with_memory_space_constraint(x, pltpu.HBM) for x in (route_ids.T, route_gates.T, tokens)])
    route, outgoing = packed[0], packed[1:]

    def hop(x, k):
        return lax.ppermute(x, "expert", [(i, i ^ k) for i in range(groups)])

    def swap(x):
        return lax.ppermute(x, "dp", [(0, 1), (1, 0)])

    order = [1, 2, 4, 5, 6, 3, 7]
    incoming = {0: outgoing[0]}
    for k in order:
        held = outgoing[k]
        if k in (3, 7):
            held, _ = lax.optimization_barrier((held, incoming[1]))
        incoming[k] = hop(held, k)
    route_now, _, _ = lax.optimization_barrier((route, incoming[1], incoming[2]))

    share = jax.ShapeDtypeStruct((half, width), bf16)
    turned = jax.ShapeDtypeStruct((width, half), bf16)
    pieces = 3 * local_experts
    weights = pl.pallas_call(
        functools.partial(load_kernel, half),
        out_shape=[turned, turned, share] * local_experts,
        in_specs=[smem] + whole(1) + [hbm] * 3,
        out_specs=whole(pieces),
        scratch_shapes=[VMEM((3, half, width), bf16), pltpu.SemaphoreType.DMA((pieces,))],
        compiler_params=params(4 + 3 * 3),
        cost_estimate=cost(0, 6 * local_experts * half * width),
        name="load",
    )(place, route_now, gate_rows, up_rows, down_weight)
    incoming[4], gate_now = lax.optimization_barrier((incoming[4], weights[0]))
    weights = [gate_now] + list(weights[1:])

    tall = groups * CAP * local_experts
    splits = 4
    part_rows = jax.ShapeDtypeStruct((tall // splits, width), bf16)
    mine = pl.pallas_call(
        functools.partial(regroup_kernel, local_experts, groups),
        out_shape=[part_rows] * splits,
        in_specs=whole(groups),
        out_specs=whole(splits),
        scratch_shapes=[VMEM((groups * block, width), bf16)],
        compiler_params=params(4),
        cost_estimate=cost(2 * tall * groups * block * width, 4 * tall * width),
        name="regroup",
    )(*[incoming[k] for k in range(groups)])
    own, other = [], []
    for h in range(splits):
        theirs = swap(mine[h])
        kept, send = pl.pallas_call(
            functools.partial(ffn_kernel, groups * CAP),
            out_shape=[jax.ShapeDtypeStruct((tall // splits, width), jnp.float32), part_rows],
            in_specs=whole(2 + pieces // splits),
            out_specs=whole(2),
            compiler_params=params(8),
            cost_estimate=cost(12 * tall * width * half // splits, 6 * local_experts * half * width // splits),
            name="ffn",
        )(mine[h], theirs, *weights[h * pieces // splits : (h + 1) * pieces // splits])
        own.append(kept)
        other.append(swap(send))
    blocks = pl.pallas_call(
        functools.partial(ungroup_kernel, local_experts, groups),
        out_shape=[jax.ShapeDtypeStruct((block, width), bf16)] * groups,
        in_specs=whole(2 * splits),
        out_specs=whole(groups),
        compiler_params=params(4),
        cost_estimate=cost(2 * tall * groups * block * width, 4 * tall * width),
        name="ungroup",
    )(*own, *other)
    returned = {k: hop(blocks[k], k) if k else blocks[k] for k in [0] + order}

    total = None
    parts = [[0, 1, 6, 7], [2, 3, 4, 5]]
    for chunk in parts:
        first, final = total is None, chunk is parts[-1]
        count = len(chunk)
        total = pl.pallas_call(
            functools.partial(combine_kernel, block, chunk, first),
            out_shape=jax.ShapeDtypeStruct((rows, width), bf16 if final else jnp.float32),
            in_specs=whole(1 + count + (not first)),
            out_specs=whole(1)[0],
            scratch_shapes=[VMEM((count * block, width), bf16)],
            compiler_params=params(4),
            cost_estimate=cost(4 * rows * count * block * width, 4 * rows * width),
            name="combine",
        )(route, *[returned[k] for k in chunk], *([] if first else [total]))
    return total


def on_device(tokens, route_ids, route_gates, gate_weight, up_weight, down_weight):
    suits = (
        lax.axis_size("expert") == 8
        and lax.axis_size("dp") == 2
        and down_weight.shape[1] == FF
        and gate_weight.shape[0] == 4
        and tokens.shape[0] == 128
    )
    run = fast if suits else general
    return run(tokens, route_ids, route_gates, gate_weight, up_weight, down_weight)


def solution(mesh):
    placed = (
        P(("parts", "expert", "dp"), None),
        P(("parts", "expert", "dp"), None),
        P(("parts", "expert", "dp"), None),
        P("expert", None, "dp"),
        P("expert", None, "dp"),
        P("expert", None, None),
    )
    return jax.shard_map(
        on_device,
        mesh=mesh,
        in_specs=placed,
        out_specs=P(("parts", "expert", "dp"), None),
        check_vma=False,
    )
```
